256 devices in a mesh: kv: 32 (over z, y), tp: 8 (over x, core).
Axes of the slice: x: 4, y: 4, z: 8, core: 2. Of those that a mesh axis runs over, the one named last changes fastest.
Arguments:
- queries: bfloat16 [8, 4, 128, 128], P(None, None, 'tp'), may hold values from -30 to 30
- cache_keys: bfloat16 [8, 8192, 8, 128], P(None, 'kv', 'tp'), may hold values from -4 to 4
- cache_values: bfloat16 [8, 8192, 8, 128], P(None, 'kv', 'tp'), may hold values from -6 to 6
- new_keys: bfloat16 [8, 4, 8, 128], P(None, None, 'tp'), may hold values from -6 to 6
- new_values: bfloat16 [8, 4, 8, 128], P(None, None, 'tp'), may hold values from -6 to 6
- lengths: int32 [8], replicated, may hold values from 512 to 8192
- residual: bfloat16 [32, 16384], P(None, 'kv'), may hold values from -4 to 4
- out_weight: bfloat16 [16384, 16384], P('tp', 'kv'), may hold values from -0.1875 to 0.1875
- norm_gain: bfloat16 [16384], P('kv'), may hold values from 0.099609375 to 1.8984375
- gate_weight: bfloat16 [16384, 26624], P('kv', 'tp'), may hold values from -0.046875 to 0.046875
- up_weight: bfloat16 [16384, 26624], P('kv', 'tp'), may hold values from -0.046875 to 0.046875
- down_weight: bfloat16 [26624, 16384], P('tp', 'kv'), may hold values from -0.0546875 to 0.0546875
Outputs:
- after_attention: bfloat16 [32, 16384], P(None, 'kv')
- layer_out: bfloat16 [32, 16384], P('tp', 'kv')
The draws below stay inside these ranges and needn't reach their ends.
All inputs are finite; a program needn't handle non-finite values.
Results may differ from the reference program's by a relative error of at most 0.019.
Values may be sent and summed in bfloat16 or wider, within the bound.
A program may use at most 64 MiB of HBM per device.

```python
import math
import jax
import jax.numpy as jnp
from jax import lax

D = 16384
HEADS = 128
KVH = 8
HD = 128
FFW = 26624
STEPS = 4
SEQS = 8
CTX = 8192
ROWS = 32


def draw_cache_keys(key, part):
    normal_key = jax.random.fold_in(key, 3)
    values = jnp.clip(jax.random.normal(normal_key, (SEQS, CTX, KVH, HD), jnp.float32), -4.0, 4.0)
    return values.astype(jnp.bfloat16)


def draw_queries(key, part):
    normal_key = jax.random.fold_in(key, 5)
    values = jnp.clip(3.0 * jax.random.normal(normal_key, (SEQS, STEPS, HEADS, HD), jnp.float32), -18.0, 18.0)
    return values.astype(jnp.bfloat16)


def draw_residual(key, part):
    normal_key = jax.random.fold_in(jax.random.fold_in(key, 9), 0)
    ramp = 0.05 * jnp.exp(math.log(20.0) * jnp.arange(D, dtype=jnp.float32)[None, :] / D)
    base = jax.random.normal(normal_key, (ROWS, D), jnp.float32)
    values = base * ramp
    return jnp.clip(values, -4.0, 4.0).astype(jnp.bfloat16)


def touch_ends(drawn, stream_key, least, top_value):
    extent = drawn.shape
    index_at = [jax.random.randint(jax.random.fold_in(stream_key, axis), (), 0, extent[axis]) for axis in range(len(extent))]
    drawn = drawn.at[tuple(index_at)].set(least)
    longest = extent.index(max(extent))
    index_at[longest] = (index_at[longest] + 1) % extent[longest]
    return drawn.at[tuple(index_at)].set(top_value)


def shard_levels(stream_key, extent, cuts, low, largest):
    def one(axis_at, shards_of):
        heights = jax.random.uniform(jax.random.fold_in(jax.random.fold_in(stream_key, 6), axis_at), (shards_of,), jnp.float32, low / len(cuts), largest / len(cuts))
        return jnp.repeat(jnp.exp(heights), extent[axis_at] // shards_of).reshape((-1,) + (1,) * (len(extent) - axis_at - 1))

    factor_of = one(*cuts[0])
    for cut in cuts[1:]:
        factor_of = factor_of * one(*cut)
    return factor_of


def noise(key, shape, scale, bound, shards=(), kind=jnp.bfloat16):
    values = jax.random.normal(key, shape, jnp.float32) * scale
    if len(shards) > 0:
        values = shard_levels(key, shape, shards, -0.22, 0.18) * values
    return jnp.clip(values, min=-bound, max=bound).astype(kind)


def setup_inputs(seed: int = 0) -> dict:
    keys = jax.random.split(jax.random.key(seed), 13)
    queries = draw_queries(jax.random.fold_in(keys[12], 71), 0)
    cache_keys = draw_cache_keys(jax.random.fold_in(keys[12], 71), 0)
    cache_values = noise(keys[2], (SEQS, CTX, KVH, HD), 1.0, 6.0, ((1, 32), (2, 8)))
    new_keys = noise(keys[3], (SEQS, STEPS, KVH, HD), 1.5, 6.0, ((2, 8),))
    new_values = noise(keys[4], (SEQS, STEPS, KVH, HD), 1.0, 6.0, ((2, 8),))
    lengths = touch_ends(jax.random.randint(keys[5], (SEQS,), CTX // 16, CTX + 1), jax.random.fold_in(keys[5], 1), CTX // 16, CTX).astype(jnp.int32)
    residual = draw_residual(jax.random.fold_in(keys[12], 71), 0)
    out_weight = noise(keys[7], (HEADS * HD, D), (HEADS * HD // 16) ** -0.5, 0.1875, ((0, 8), (1, 32)))
    norm_gain = jnp.clip(1.0 + 0.18 * jax.random.normal(keys[8], (D,), jnp.float32), 0.099609375, 1.8984375).astype(jnp.bfloat16)
    gate_weight = noise(keys[9], (D, FFW), D ** -0.5, 0.046875, ((0, 32), (1, 8)))
    up_weight = noise(keys[10], (D, FFW), D ** -0.5, 0.046875, ((0, 32), (1, 8)))
    down_weight = noise(keys[11], (FFW, D), (FFW // 2) ** -0.5, 0.0546875, ((0, 8), (1, 32)))
    return {"queries": queries, "cache_keys": cache_keys, "cache_values": cache_values, "new_keys": new_keys, "new_values": new_values, "lengths": lengths, "residual": residual, "out_weight": out_weight, "norm_gain": norm_gain, "gate_weight": gate_weight, "up_weight": up_weight, "down_weight": down_weight}


def reference(queries, cache_keys, cache_values, new_keys, new_values, lengths, residual, out_weight, norm_gain, gate_weight, up_weight, down_weight):
    group_size = HEADS // KVH
    scaling = 1.0 / math.sqrt(HD)
    grouped = queries.astype(jnp.float32).reshape(SEQS, STEPS, KVH, group_size, HD)
    cache_scores = jnp.einsum('stgjd,scgd->sgjtc', grouped, cache_keys.astype(jnp.float32)) * scaling
    fresh_scores = jnp.einsum('stgjd,sugd->sgjtu', grouped, new_keys.astype(jnp.float32)) * scaling
    position = jnp.arange(CTX, dtype=jnp.int32)
    in_range = (position[None, :] < lengths[:, None])[:, None, None, None, :]
    causal = jnp.arange(STEPS, dtype=jnp.int32)[:, None] >= jnp.arange(STEPS, dtype=jnp.int32)[None, :]
    cache_masked = jnp.where(in_range, cache_scores, -1e+30)
    fresh_masked = jnp.where(causal, fresh_scores, -1e+30)
    row_max = jnp.maximum(lax.optimization_barrier(jnp.max(cache_masked, axis=-1)), lax.optimization_barrier(jnp.max(fresh_masked, axis=-1)))
    cache_weights = jnp.where(in_range, jnp.exp(cache_masked - row_max[..., None]), 0.0)
    fresh_weights = jnp.where(causal, jnp.exp(fresh_masked - row_max[..., None]), 0.0)
    denominator = lax.optimization_barrier(jnp.sum(cache_weights, axis=-1)) + lax.optimization_barrier(jnp.sum(fresh_weights, axis=-1))
    cache_rounded = lax.optimization_barrier(cache_weights.astype(jnp.bfloat16)).astype(jnp.float32)
    fresh_rounded = lax.optimization_barrier(fresh_weights.astype(jnp.bfloat16)).astype(jnp.float32)
    numerator = jnp.einsum('sgjtc,scgd->sgjtd', cache_rounded, cache_values.astype(jnp.float32))
    numerator = numerator + jnp.einsum('sgjtu,sugd->sgjtd', fresh_rounded, new_values.astype(jnp.float32))
    attended = (numerator / denominator[..., None]).transpose(0, 3, 1, 2, 4).reshape(ROWS, HEADS * HD).astype(jnp.bfloat16)
    projected = jnp.dot(attended, out_weight, preferred_element_type=jnp.float32)
    after_attention = (residual.astype(jnp.float32) + projected).astype(jnp.bfloat16)
    wide_rows = lax.optimization_barrier(after_attention).astype(jnp.float32)
    inverse = lax.rsqrt(lax.optimization_barrier(jnp.mean(wide_rows * wide_rows, axis=1)) + 1e-05)
    normed = (wide_rows * norm_gain.astype(jnp.float32)[None, :] * inverse[:, None]).astype(jnp.bfloat16)
    gate = jnp.dot(normed, gate_weight, preferred_element_type=jnp.float32)
    upward = jnp.dot(normed, up_weight, preferred_element_type=jnp.float32)
    hidden = (jax.nn.silu(gate) * upward).astype(jnp.bfloat16)
    layer_out = (wide_rows + jnp.dot(hidden, down_weight, preferred_element_type=jnp.float32)).astype(jnp.bfloat16)
    return (after_attention, layer_out)
```

```python
import math

import jax
import jax.numpy as jnp
from jax import lax
from jax.experimental import pallas as pl
from jax.experimental.pallas import tpu as pltpu
from jax.sharding import PartitionSpec as P

F32, BF16 = jnp.float32, jnp.bfloat16
MESH = pl.DeviceIdType.MESH
Z, Y, TP = 8, 4, 8
KV = Z * Y
SEQS, STEPS, HEADS, HD = 8, 4, 16, 128
CTX = 256
COLS = 512
MODEL = 16384
FF = 3328
WIDTH = (3, 3, 3, 3, 3, 3, 4, 4)
START = tuple(sum(WIDTH[:c]) * 128 for c in range(Z))
SCALE = 1.0 / math.sqrt(HD)
LOW = -1e30


def drain(ref, sem):
    pltpu.make_async_copy(ref, ref, sem).wait()


def kernel(
    lengths,
    q_in, k_in, v_in, nk_in, nv_in, res_in, wo_in, gain_in, wg_in, wu_in, wd_in,
    after_out, layer_out,
    qv, kb, vb, nkb, nvb, resb, wo, gainb, wg, wu, wd,
    obuf, sbuf, ra, rs, tb, gb, gf, pr, aft,
    sqb, sqr, sqz, yb, yr, zs, zr, hr, fs, fr,
    load_sem, a_send, a_recv, b_send, b_recv, c_send, c_recv,
    y_send, y_recv, sq_send, sq_recv, z_send, z_recv,
    hz_send, hz_recv, hy_send, hy_recv, f_send, f_recv,
):
    kv, tp = lax.axis_index("kv"), lax.axis_index("tp")
    z, y = kv // Y, kv % Y
    x, core = tp // 2, tp % 2

    pairs = (
        (q_in, qv), (k_in, kb), (v_in, vb), (nk_in, nkb), (nv_in, nvb), (res_in, resb), (gain_in, gainb),
        (wo_in, wo), (wg_in, wg), (wu_in, wu), (wd_in, wd),
    )
    loads = [pltpu.make_async_copy(a, b, load_sem.at[i]) for i, (a, b) in enumerate(pairs)]
    for copy in loads:
        copy.start()
    l_q, l_k, l_v, l_nk, l_nv, l_res, l_gain, l_wo, l_wg, l_wu, l_wd = loads

    def send(src, dst, send_sem, recv_sem, to):
        pltpu.make_async_remote_copy(
            src_ref=src, dst_ref=dst, send_sem=send_sem, recv_sem=recv_sem, device_id=to, device_id_type=MESH
        ).start()

    barrier = pltpu.get_barrier_semaphore()

    @pl.loop(1, KV)
    def _(i):
        pl.semaphore_signal(barrier, inc=1, device_id=(lax.rem(kv + i, KV), tp), device_id_type=MESH)

    @pl.loop(1, TP)
    def _(i):
        pl.semaphore_signal(barrier, inc=1, device_id=(kv, lax.rem(tp + i, TP)), device_id_type=MESH)

    l_q.wait()
    l_k.wait()
    l_v.wait()
    position = lax.broadcasted_iota(jnp.int32, (STEPS * HEADS, CTX), 1) + kv * CTX
    lane = lax.broadcasted_iota(jnp.int32, (128, 128), 1)
    stats = jnp.zeros((128, 128), F32)
    for s in range(SEQS):
        rows = qv[s * STEPS : (s + 1) * STEPS].reshape(STEPS * HEADS, HD)
        scores = lax.dot_general(rows, kb[s], (((1,), (1,)), ((), ())), preferred_element_type=F32) * SCALE
        inside = position < lengths[s]
        scores = jnp.where(inside, scores, LOW)
        top = jnp.max(scores, axis=1, keepdims=True)
        weights = jnp.where(inside, jnp.exp(scores - top), 0.0)
        total = jnp.sum(weights, axis=1, keepdims=True)
        sums = jnp.dot(weights.astype(BF16), vb[s], preferred_element_type=F32)
        obuf[s * STEPS : (s + 1) * STEPS] = sums.reshape(STEPS, HEADS, HD).astype(BF16)
        stats = jnp.where(lane == s, jnp.concatenate([top, total], axis=0), stats)
    turned = stats.T
    for s in range(SEQS):
        sbuf[s] = turned[s : s + 1]

    pl.semaphore_wait(barrier, KV - 1 + TP - 1)

    @pl.loop(1, KV)
    def _(i):
        to = lax.rem(kv + i, KV)
        send(sbuf.at[to // Y], rs.at[KV - 1 - i], a_send.at[0], a_recv.at[0], (to, tp))
        send(obuf.at[to], ra.at[KV - 1 - i], a_send.at[1], a_recv.at[1], (to, tp))

    l_nk.wait()
    l_nv.wait()
    own_q = qv[kv].astype(F32)
    fresh_k, fresh_v = nkb[z].astype(F32), nvb[z].astype(F32)
    fresh = []
    for u in range(STEPS):
        score = jnp.sum(own_q * fresh_k[u : u + 1], axis=1, keepdims=True) * SCALE
        fresh.append(jnp.where(u <= y, score, LOW))
    rs[KV - 1] = sbuf[z]
    drain(rs.at[0 : KV - 1], a_recv.at[0])
    tb[:, 0:KV] = rs[...].reshape(KV, 128).T
    tops = tb[pl.ds(pl.multiple_of(y * HEADS, HEADS), HEADS), 0:KV]
    totals = tb[pl.ds(pl.multiple_of(64 + y * HEADS, HEADS), HEADS), 0:KV]
    row_max = jnp.max(tops, axis=1, keepdims=True)
    for score in fresh:
        row_max = jnp.maximum(row_max, score)
    factor = jnp.exp(tops - row_max)
    denominator = jnp.sum(factor * totals, axis=1, keepdims=True)
    numerator = factor[:, KV - 1 : KV] * obuf[kv].astype(F32)
    for u in range(STEPS):
        weight = jnp.where(u <= y, jnp.exp(fresh[u] - row_max), 0.0)
        denominator += weight
        numerator += weight.astype(BF16).astype(F32) * fresh_v[u : u + 1]
    drain(ra, a_recv.at[1])
    for j in range(KV - 1):
        numerator += factor[:, j : j + 1] * ra[j].astype(F32)
    gb[kv] = (numerator / denominator).astype(BF16)

    @pl.loop(1, KV)
    def _(i):
        to = lax.rem(kv + i, KV)
        send(gb.at[kv], gb.at[kv], b_send, b_recv, (to, tp))

    l_wo.wait()
    l_res.wait()
    l_gain.wait()
    drain(gb.at[0 : KV - 1], b_recv)
    gf[...] = gb[...].astype(F32).reshape(KV * HEADS, HD)
    attended = jnp.concatenate(
        [gf[pl.ds(h, KV, stride=HEADS), :].astype(BF16) for h in range(HEADS)], axis=1
    )
    pr[tp] = jnp.dot(attended, wo[...], preferred_element_type=F32).astype(BF16)

    @pl.loop(1, TP)
    def _(i):
        send(pr.at[tp], pr.at[tp], c_send, c_recv, (kv, lax.rem(tp + i, TP)))

    drain(pr.at[0 : TP - 1], c_recv)
    summed = resb[...].astype(F32)
    for t in range(TP):
        summed += pr[t].astype(F32)
    after = summed.astype(BF16)
    after_out[...] = after
    wide = after.astype(F32)
    aft[...] = wide

    sqb[...] = jnp.broadcast_to(jnp.sum(wide * wide, axis=1, keepdims=True), (KV, 128)).reshape(Y, 8, 128)

    def over_y(body):
        for i in range(1, Y):
            p = lax.rem(y + i, Y)
            body(p, Y - 1 - i, (z * Y + p, tp))

    def over_z(body):
        for i in range(1, Z):
            p = lax.rem(z + i, Z)
            body((p * Y + y, tp))

    over_y(lambda p, slot, to: send(sqb.at[p], sqr.at[slot], sq_send.at[0], sq_recv.at[0], to))
    normed = (wide * gainb[...].astype(F32)).astype(BF16)

    def finish_y(c):
        n = WIDTH[c] * 256
        drain(yr.at[c, :, :, 0:n], y_recv.at[c])
        part = yb[c, y, :, 0:n].astype(F32)
        for i in range(Y - 1):
            part += yr[c, i, :, 0:n].astype(F32)
        zs[c, :, 0:n] = part.astype(BF16)

        @pl.when(z != c)
        def _():
            send(zs.at[c, :, 0:n], zr.at[z, :, 0:n], z_send.at[c], z_recv, (c * Y + y, tp))

    l_wg.wait()
    l_wu.wait()
    lag = 3
    for c in range(Z):
        n, at = WIDTH[c], START[c]
        gate = jnp.dot(normed, wg[:, at : at + n * 128], preferred_element_type=F32)
        up = jnp.dot(normed, wu[:, at : at + n * 128], preferred_element_type=F32)
        for j in range(n):
            for half, value in enumerate((gate, up)):
                tile = value[:, j * 128 : (j + 1) * 128].reshape(Y, 8, 128)
                yb[c, :, :, j * 256 + half * 128 : j * 256 + half * 128 + 128] = tile.astype(BF16)
        over_y(
            lambda p, slot, to: send(
                yb.at[c, p, :, 0 : n * 256], yr.at[c, slot, :, 0 : n * 256], y_send.at[c], y_recv.at[c], to
            )
        )
        if c == lag - 1:
            drain(sqr, sq_recv.at[0])
            sqz[z] = sqb[y] + sqr[0] + sqr[1] + sqr[2]
            over_z(lambda to: send(sqz.at[z], sqz.at[z], sq_send.at[1], sq_recv.at[1], to))
        if c >= lag:
            finish_y(c - lag)
    for c in range(Z - lag, Z):
        finish_y(c)

    zr[z] = zs[z]
    drain(sqz.at[0 : Z - 1], sq_recv.at[1])
    squares = sqz[0]
    for i in range(1, Z):
        squares += sqz[i]
    inverse = lax.rsqrt(squares / MODEL + 1e-05)

    @pl.when(z < 6)
    def _():
        drain(zr.at[0 : Z - 1, :, 0:768], z_recv)

    @pl.when(z >= 6)
    def _():
        drain(zr.at[0 : Z - 1, :, 0:1024], z_recv)

    both = zr[0].astype(F32)
    for i in range(1, Z):
        both += zr[i].astype(F32)
    for j in range(4):
        gate = both[:, j * 256 : j * 256 + 128] * inverse
        up = both[:, j * 256 + 128 : j * 256 + 256] * inverse
        hr[z, y, :, j * 128 : (j + 1) * 128] = (gate / (1.0 + jnp.exp(-gate)) * up).astype(BF16)

    def send_hidden(n):
        own = hr.at[z, y, :, 0:n]
        over_z(lambda to: send(own, own, hz_send, hz_recv.at[z], to))
        over_y(lambda p, slot, to: send(own, own, hy_send.at[z], hy_recv.at[z], to))

    @pl.when(z < 6)
    def _():
        send_hidden(384)

    @pl.when(z >= 6)
    def _():
        send_hidden(512)

    for c in range(Z):
        n = WIDTH[c] * 128

        @pl.when(z != c)
        def _():
            piece = hr.at[c, y, :, 0:n]
            drain(piece, hz_recv.at[c])
            over_y(lambda p, slot, to: send(piece, piece, hy_send.at[c], hy_recv.at[c], to))

    l_wd.wait()
    down = jnp.zeros((KV, COLS), F32)
    for c in range(Z):
        n = WIDTH[c] * 128
        drain(hr.at[c, 0 : Y - 1, :, 0:n], hy_recv.at[c])
        hidden = hr[c, :, :, 0:n].astype(F32).reshape(KV, n).astype(BF16)
        down += jnp.dot(hidden, wd[START[c] : START[c] + n, :], preferred_element_type=F32)
    fs[...] = down.reshape(4, 8, COLS).astype(BF16)

    @pl.loop(1, TP)
    def _(i):
        to = lax.rem(tp + i, TP)
        send(fs.at[to // 2], fr.at[TP - 1 - i], f_send, f_recv, (kv, to))

    rows = aft[pl.ds(pl.multiple_of(x * 8, 8), 8), :] + fs[x].astype(F32)
    drain(fr, f_recv)
    for i in range(TP - 1):
        rows += fr[i].astype(F32)
    layer_out[...] = jnp.where(core == 0, rows[0:4], rows[4:8]).astype(BF16)

    drain(rs.at[0 : KV - 1], a_send.at[0])
    drain(ra, a_send.at[1])
    drain(gb.at[0 : KV - 1], b_send)
    drain(pr.at[0 : TP - 1], c_send)
    drain(sqr, sq_send.at[0])
    drain(sqz.at[0 : Z - 1], sq_send.at[1])
    for c in range(Z):
        n = WIDTH[c] * 128
        drain(yr.at[c, :, :, 0 : 2 * n], y_send.at[c])
        drain(hr.at[c, 0 : Y - 1, :, 0:n], hy_send.at[c])

        @pl.when(z != c)
        def _():
            drain(zs.at[c, :, 0 : 2 * n], z_send.at[c])

    @pl.when(z < 6)
    def _():
        drain(hr.at[0 : Z - 1, 0, :, 0:384], hz_send)

    @pl.when(z >= 6)
    def _():
        drain(hr.at[0 : Z - 1, 0, :, 0:512], hz_send)

    drain(fr, f_send)


def local(queries, cache_keys, cache_values, new_keys, new_values, lengths, residual, out_weight, norm_gain,
          gate_weight, up_weight, down_weight):
    hbm = pl.BlockSpec(memory_space=pl.ANY)
    vmem = pl.BlockSpec(memory_space=pltpu.VMEM)
    dma = pltpu.SemaphoreType.DMA
    return pl.pallas_call(
        kernel,
        out_shape=(jax.ShapeDtypeStruct((KV, COLS), BF16), jax.ShapeDtypeStruct((4, COLS), BF16)),
        in_specs=[pl.BlockSpec(memory_space=pltpu.SMEM)] + [hbm] * 11,
        out_specs=(vmem, vmem),
        scratch_shapes=[
            pltpu.VMEM((KV, HEADS, HD), BF16),
            pltpu.VMEM((SEQS, CTX, HD), BF16),
            pltpu.VMEM((SEQS, CTX, HD), BF16),
            pltpu.VMEM((SEQS, STEPS, HD), BF16),
            pltpu.VMEM((SEQS, STEPS, HD), BF16),
            pltpu.VMEM((KV, COLS), BF16),
            pltpu.VMEM((HEADS * HD, COLS), BF16),
            pltpu.VMEM((1, COLS), F32),
            pltpu.VMEM((COLS, FF), BF16),
            pltpu.VMEM((COLS, FF), BF16),
            pltpu.VMEM((FF, COLS), BF16),
            pltpu.VMEM((KV, HEADS, HD), BF16),
            pltpu.VMEM((SEQS, 1, 128), F32),
            pltpu.VMEM((KV - 1, HEADS, HD), BF16),
            pltpu.VMEM((KV, 1, 128), F32),
            pltpu.VMEM((128, 128), F32),
            pltpu.VMEM((KV, HEADS, HD), BF16),
            pltpu.VMEM((KV * HEADS, HD), F32),
            pltpu.VMEM((TP, KV, COLS), BF16),
            pltpu.VMEM((KV, COLS), F32),
            pltpu.VMEM((Y, 8, 128), F32),
            pltpu.VMEM((Y - 1, 8, 128), F32),
            pltpu.VMEM((Z, 8, 128), F32),
            pltpu.VMEM((Z, Y, 8, 1024), BF16),
            pltpu.VMEM((Z, Y - 1, 8, 1024), BF16),
            pltpu.VMEM((Z, 8, 1024), BF16),
            pltpu.VMEM((Z, 8, 1024), BF16),
            pltpu.VMEM((Z, Y, 8, 512), BF16),
            pltpu.VMEM((4, 8, COLS), BF16),
            pltpu.VMEM((TP - 1, 8, COLS), BF16),
            dma((11,)), dma((2,)), dma((2,)), dma, dma, dma, dma,
            dma((Z,)), dma((Z,)), dma((2,)), dma((2,)), dma((Z,)), dma,
            dma, dma((Z,)), dma((Z,)), dma((Z,)), dma, dma,
        ],
        compiler_params=pltpu.CompilerParams(
            collective_id=0, has_side_effects=True, vmem_limit_bytes=60 * 1024 * 1024
        ),
    )(
        lengths,
        queries.reshape(KV, HEADS, HD),
        cache_keys.reshape(SEQS, CTX, HD),
        cache_values.reshape(SEQS, CTX, HD),
        new_keys.reshape(SEQS, STEPS, HD),
        new_values.reshape(SEQS, STEPS, HD),
        residual,
        out_weight,
        norm_gain.astype(F32).reshape(1, COLS),
        gate_weight,
        up_weight,
        down_weight,
    )


def solution(mesh):
    return jax.shard_map(
        local,
        mesh=mesh,
        in_specs=(
            P(None, None, "tp", None),
            P(None, "kv", "tp", None),
            P(None, "kv", "tp", None),
            P(None, None, "tp", None),
            P(None, None, "tp", None),
            P(),
            P(None, "kv"),
            P("tp", "kv"),
            P("kv"),
            P("kv", "tp"),
            P("kv", "tp"),
            P("tp", "kv"),
        ),
        out_specs=(P(None, "kv"), P("tp", "kv")),
        check_vma=False,
    )
```

```python
import math

import jax
import jax.numpy as jnp
from jax import lax
from jax.experimental import pallas as pl
from jax.experimental.pallas import tpu as pltpu
from jax.sharding import PartitionSpec as P

F32, BF16 = jnp.float32, jnp.bfloat16
MESH = pl.DeviceIdType.MESH
Z, Y, TP = 8, 4, 8
KV = Z * Y
SEQS, STEPS, HEADS, HD = 8, 4, 16, 128
CTX = 256
COLS = 512
MODEL = 16384
FF = 3328
FAR_FIRST = (4, 3, 5, 2, 6, 1, 7, 0)
HOPS = lambda o: min(o[0], Z - o[0]) + min(o[1], Y - o[1])
OTHERS = sorted(((d, e) for d in range(Z) for e in range(Y) if d or e), key=HOPS, reverse=True)


def slot_of(d, e):
    return (Z - d) % Z * Y + (Y - e) % Y - 1


SCALE = 1.0 / math.sqrt(HD)
LOW = -1e30


def drain(ref, sem):
    pltpu.make_async_copy(ref, ref, sem).wait()


def by_width(c, body):
    @pl.when(c < 6)
    def _():
        body(3)

    @pl.when(c >= 6)
    def _():
        body(4)


def start_of(c):
    return pl.multiple_of(c * 384 + jnp.maximum(c - 6, 0) * 128, 128)


def kernel(
    lengths_in,
    q_in, k_in, v_in, nk_in, nv_in, res_in, wo_in, gain_in, wg_in, wu_in, wd_in,
    after_out, layer_out,
    lengths, qv, kb, vb, nkb, nvb, resb, wo, gainb, wg, wu, wd,
    obuf, sbuf, ra, rs, tb, gb, gf, pr, aft,
    aftb, sq, yb, yr, own_sum, zs, zr, hr, hsent, down_sum, fs, fr, lastb,
    load_sem, a_send, a_recv, b_send, b_recv, c_send, c_recv,
    sq_send, sq_recv, y_send, y_recv, z_send, z_recv, h_send, h_recv, f_send, f_recv, out_sem,
):
    kv, tp = lax.axis_index("kv"), lax.axis_index("tp")
    z, y = kv // Y, kv % Y
    x, core = tp // 2, tp % 2

    barrier = pltpu.get_barrier_semaphore()

    @pl.loop(1, KV)
    def _(i):
        pl.semaphore_signal(barrier, inc=1, device_id=(lax.rem(kv + i, KV), tp), device_id_type=MESH)

    @pl.loop(1, TP)
    def _(i):
        pl.semaphore_signal(barrier, inc=1, device_id=(kv, lax.rem(tp + i, TP)), device_id_type=MESH)

    pairs = (
        (lengths_in, lengths), (q_in, qv), (k_in, kb), (v_in, vb), (nk_in, nkb), (nv_in, nvb), (res_in, resb), (gain_in, gainb),
        (wo_in, wo), (wg_in, wg), (wu_in, wu), (wd_in, wd),
    )
    loads = [pltpu.make_async_copy(a, b, load_sem.at[i]) for i, (a, b) in enumerate(pairs)]
    for copy in loads:
        copy.start()
    l_len, l_q, l_k, l_v, l_nk, l_nv, l_res, l_gain, l_wo, l_wg, l_wu, l_wd = loads

    def send(src, dst, send_sem, recv_sem, to):
        pltpu.make_async_remote_copy(
            src_ref=src, dst_ref=dst, send_sem=send_sem, recv_sem=recv_sem, device_id=to, device_id_type=MESH
        ).start()

    def of_plane(d, e):
        return lax.rem(z + d, Z) * Y + lax.rem(y + e, Y)

    l_len.wait()
    l_q.wait()
    l_k.wait()
    l_v.wait()
    position = lax.broadcasted_iota(jnp.int32, (STEPS * HEADS, CTX), 1) + kv * CTX
    lane = lax.broadcasted_iota(jnp.int32, (128, 128), 1)
    stats = jnp.zeros((128, 128), F32)
    for s in range(SEQS):
        rows = qv[s * STEPS : (s + 1) * STEPS].reshape(STEPS * HEADS, HD)
        scores = lax.dot_general(rows, kb[s], (((1,), (1,)), ((), ())), preferred_element_type=F32) * SCALE
        inside = position < lengths[s]
        scores = jnp.where(inside, scores, LOW)
        top = jnp.max(scores, axis=1, keepdims=True)
        weights = jnp.where(inside, jnp.exp(scores - top), 0.0)
        total = jnp.sum(weights, axis=1, keepdims=True)
        sums = jnp.dot(weights.astype(BF16), vb[s], preferred_element_type=F32)
        obuf[s * STEPS : (s + 1) * STEPS] = sums.reshape(STEPS, HEADS, HD).astype(BF16)
        stats = jnp.where(lane == s, jnp.concatenate([top, total], axis=0), stats)
    turned = stats.T
    for s in range(SEQS):
        sbuf[s] = turned[s : s + 1]

    pl.semaphore_wait(barrier, KV - 1 + TP - 1)

    for d, e in OTHERS:
        to = of_plane(d, e)
        send(sbuf.at[to // Y], rs.at[slot_of(d, e)], a_send.at[0], a_recv.at[0], (to, tp))
        send(obuf.at[to], ra.at[slot_of(d, e)], a_send.at[1], a_recv.at[1], (to, tp))

    l_nk.wait()
    l_nv.wait()
    own_q = qv[kv].astype(F32)
    fresh_k, fresh_v = nkb[z].astype(F32), nvb[z].astype(F32)
    fresh = []
    for u in range(STEPS):
        score = jnp.sum(own_q * fresh_k[u : u + 1], axis=1, keepdims=True) * SCALE
        fresh.append(jnp.where(u <= y, score, LOW))
    rs[KV - 1] = sbuf[z]
    drain(rs.at[0 : KV - 1], a_recv.at[0])
    tb[:, 0:KV] = rs[...].reshape(KV, 128).T
    tops = tb[pl.ds(pl.multiple_of(y * HEADS, HEADS), HEADS), 0:KV]
    totals = tb[pl.ds(pl.multiple_of(64 + y * HEADS, HEADS), HEADS), 0:KV]
    row_max = jnp.max(tops, axis=1, keepdims=True)
    for score in fresh:
        row_max = jnp.maximum(row_max, score)
    factor = jnp.exp(tops - row_max)
    denominator = jnp.sum(factor * totals, axis=1, keepdims=True)
    numerator = factor[:, KV - 1 : KV] * obuf[kv].astype(F32)
    for u in range(STEPS):
        weight = jnp.where(u <= y, jnp.exp(fresh[u] - row_max), 0.0)
        denominator += weight
        numerator += weight.astype(BF16).astype(F32) * fresh_v[u : u + 1]
    drain(ra, a_recv.at[1])
    for j in range(KV - 1):
        numerator += factor[:, j : j + 1] * ra[j].astype(F32)
    gb[kv] = (numerator / denominator).astype(BF16)

    for d, e in OTHERS:
        send(gb.at[kv], gb.at[kv], b_send, b_recv, (of_plane(d, e), tp))

    l_wo.wait()
    l_res.wait()
    l_gain.wait()
    drain(gb.at[0 : KV - 1], b_recv)
    gf[...] = gb[...].astype(F32).reshape(KV * HEADS, HD)
    attended = jnp.concatenate(
        [gf[pl.ds(h, KV, stride=HEADS), :].astype(BF16) for h in range(HEADS)], axis=1
    )
    pr[tp] = jnp.dot(attended, wo[...], preferred_element_type=F32).astype(BF16)

    for i in FAR_FIRST[:-1]:
        send(pr.at[tp], pr.at[tp], c_send, c_recv, (kv, lax.rem(tp + i, TP)))

    drain(pr.at[0 : TP - 1], c_recv)
    summed = resb[...].astype(F32)
    for t in range(TP):
        summed += pr[t].astype(F32)
    after = summed.astype(BF16)
    wide = after.astype(F32)
    aft[...] = wide
    aftb[...] = after
    put_after = pltpu.make_async_copy(aftb, after_out, out_sem.at[0])
    put_after.start()

    squares = jnp.broadcast_to(jnp.sum(wide * wide, axis=1, keepdims=True), (KV, 128)).T
    sq[KV - 1, :, 0:KV] = squares[0:1]
    for d, e in OTHERS:
        send(sq.at[KV - 1], sq.at[slot_of(d, e)], sq_send, sq_recv, (of_plane(d, e), tp))

    normed = jnp.concatenate(
        [wide[:, j * 128 : (j + 1) * 128] * gainb[j : j + 1].astype(F32) for j in range(COLS // 128)], axis=1
    ).astype(BF16)

    def multiply(d):
        c = lax.rem(z + d, Z)

        def body(n):
            gate = jnp.dot(normed, wg[:, pl.ds(start_of(c), n * 128)], preferred_element_type=F32)
            up = jnp.dot(normed, wu[:, pl.ds(start_of(c), n * 128)], preferred_element_type=F32)
            for i in range(n):
                for half, value in enumerate((gate, up)):
                    tile = value[:, i * 128 : (i + 1) * 128].reshape(Y, 8, 128)
                    yb[d, :, :, i * 256 + half * 128 : i * 256 + half * 128 + 128] = tile.astype(BF16)
            for e in (2, 1, 3):
                send(
                    yb.at[d, lax.rem(y + e, Y), :, 0 : n * 256],
                    yr.at[d, Y - 1 - e, :, 0 : n * 256],
                    y_send.at[d],
                    y_recv.at[d],
                    (of_plane(0, e), tp),
                )

        by_width(c, body)

    l_wg.wait()
    l_wu.wait()
    for d in FAR_FIRST:
        multiply(d)

    def finish_y(d):
        c = lax.rem(z + d, Z)

        def body(n):
            n = n * 256
            drain(yr.at[d, :, :, 0:n], y_recv.at[d])
            part = yb[d, y, :, 0:n].astype(F32)
            for i in range(Y - 1):
                part += yr[d, i, :, 0:n].astype(F32)
            if d == 0:
                own_sum[:, 0:n] = part
            else:
                zs[d, :, 0:n] = part.astype(BF16)
                send(zs.at[d, :, 0:n], zr.at[Z - 1 - d, :, 0:n], z_send.at[d], z_recv, (of_plane(d, 0), tp))

        by_width(c, body)

    for d in FAR_FIRST:
        finish_y(d)

    drain(sq.at[0 : KV - 1], sq_recv)
    tb[...] = jnp.broadcast_to(jnp.sum(sq[...].reshape(KV, 128), axis=0, keepdims=True), (128, 128)).T
    inverse = lax.rsqrt(tb[pl.ds(pl.multiple_of(y * 8, 8), 8), :] / MODEL + 1e-05)

    by_width(z, lambda n: drain(zr.at[:, :, 0 : n * 256], z_recv))
    both = own_sum[...]
    for i in range(Z - 1):
        both += zr[i].astype(F32)
    for j in range(4):
        gate = both[:, j * 256 : j * 256 + 128] * inverse
        up = both[:, j * 256 + 128 : j * 256 + 256] * inverse
        hr[z, y, :, j * 128 : (j + 1) * 128] = (gate / (1.0 + jnp.exp(-gate)) * up).astype(BF16)

    def send_hidden(n):
        own = hr.at[z, y, :, 0 : n * 128]
        for d, e in OTHERS:
            send(own, own, h_send, h_recv.at[(Z - d) % Z], (of_plane(d, e), tp))

    by_width(z, send_hidden)

    def multiply_down(d):
        c = lax.rem(z + d, Z)

        def body(n):
            drain(hr.at[c, 0 : Y - (d == 0), :, 0 : n * 128], h_recv.at[d])
            hidden = hr[c, :, :, 0 : n * 128].astype(F32).reshape(KV, n * 128).astype(BF16)
            part = jnp.dot(hidden, wd[pl.ds(start_of(c), n * 128), :], preferred_element_type=F32)
            if d == 0:
                down_sum[...] = part
            else:
                down_sum[...] += part

        by_width(c, body)

    l_wd.wait()
    for d in FAR_FIRST[::-1]:
        multiply_down(d)
    down = down_sum[...]
    fs[...] = down.reshape(4, 8, COLS).astype(BF16)

    for i in FAR_FIRST[:-1]:
        to = lax.rem(tp + i, TP)
        send(fs.at[to // 2], fr.at[TP - 1 - i], f_send, f_recv, (kv, to))

    rows = aft[pl.ds(pl.multiple_of(x * 8, 8), 8), :] + fs[x].astype(F32)
    drain(fr, f_recv)
    for i in range(TP - 1):
        rows += fr[i].astype(F32)
    lastb[...] = jnp.where(core == 0, rows[0:4], rows[4:8]).astype(BF16)
    put_layer = pltpu.make_async_copy(lastb, layer_out, out_sem.at[1])
    put_layer.start()

    drain(rs.at[0 : KV - 1], a_send.at[0])
    drain(ra, a_send.at[1])
    drain(gb.at[0 : KV - 1], b_send)
    drain(pr.at[0 : TP - 1], c_send)
    drain(sq.at[0 : KV - 1], sq_send)
    for d in range(Z):

        def left(n, d=d):
            drain(yr.at[d, :, :, 0 : n * 256], y_send.at[d])
            if d:
                drain(zs.at[d, :, 0 : n * 256], z_send.at[d])

        by_width(lax.rem(z + d, Z), left)
    by_width(z, lambda n: drain(hsent.at[:, :, 0 : n * 128], h_send))
    drain(fr, f_send)
    put_after.wait()
    put_layer.wait()


def write_out(after_in, layer_in, after_out, layer_out):
    after_out[...] = after_in[...]
    layer_out[...] = layer_in[...]


def local(queries, cache_keys, cache_values, new_keys, new_values, lengths, residual, out_weight, norm_gain,
          gate_weight, up_weight, down_weight):
    hbm = pl.BlockSpec(memory_space=pl.ANY)
    vmem = pl.BlockSpec(memory_space=pltpu.VMEM)
    dma = pltpu.SemaphoreType.DMA
    after, layer = pl.pallas_call(
        kernel,
        out_shape=(jax.ShapeDtypeStruct((KV, COLS), BF16), jax.ShapeDtypeStruct((4, COLS), BF16)),
        in_specs=[hbm] * 12,
        out_specs=(hbm, hbm),
        scratch_shapes=[
            pltpu.SMEM((SEQS,), jnp.int32),
            pltpu.VMEM((KV, HEADS, HD), BF16),
            pltpu.VMEM((SEQS, CTX, HD), BF16),
            pltpu.VMEM((SEQS, CTX, HD), BF16),
            pltpu.VMEM((SEQS, STEPS, HD), BF16),
            pltpu.VMEM((SEQS, STEPS, HD), BF16),
            pltpu.VMEM((KV, COLS), BF16),
            pltpu.VMEM((HEADS * HD, COLS), BF16),
            pltpu.VMEM((4, 128), BF16),
            pltpu.VMEM((COLS, FF), BF16),
            pltpu.VMEM((COLS, FF), BF16),
            pltpu.VMEM((FF, COLS), BF16),
            pltpu.VMEM((KV, HEADS, HD), BF16),
            pltpu.VMEM((SEQS, 1, 128), F32),
            pltpu.VMEM((KV - 1, HEADS, HD), BF16),
            pltpu.VMEM((KV, 1, 128), F32),
            pltpu.VMEM((128, 128), F32),
            pltpu.VMEM((KV, HEADS, HD), BF16),
            pltpu.VMEM((KV * HEADS, HD), F32),
            pltpu.VMEM((TP, KV, COLS), BF16),
            pltpu.VMEM((KV, COLS), F32),
            pltpu.VMEM((KV, COLS), BF16),
            pltpu.VMEM((KV, 1, 128), F32),
            pltpu.VMEM((Z, Y, 8, 1024), BF16),
            pltpu.VMEM((Z, Y - 1, 8, 1024), BF16),
            pltpu.VMEM((8, 1024), F32),
            pltpu.VMEM((Z, 8, 1024), BF16),
            pltpu.VMEM((Z - 1, 8, 1024), BF16),
            pltpu.VMEM((Z, Y, 8, 512), BF16),
            pltpu.VMEM((KV - 1, 8, 512), BF16),
            pltpu.VMEM((KV, COLS), F32),
            pltpu.VMEM((4, 8, COLS), BF16),
            pltpu.VMEM((TP - 1, 8, COLS), BF16),
            pltpu.VMEM((4, COLS), BF16),
            dma((12,)), dma((2,)), dma((2,)), dma, dma, dma, dma,
            dma, dma, dma((Z,)), dma((Z,)), dma((Z,)), dma, dma, dma((Z,)), dma, dma, dma((2,)),
        ],
        compiler_params=pltpu.CompilerParams(
            collective_id=0, has_side_effects=True, vmem_limit_bytes=60 * 1024 * 1024
        ),
    )(
        lengths,
        queries.reshape(KV, HEADS, HD),
        cache_keys.reshape(SEQS, CTX, HD),
        cache_values.reshape(SEQS, CTX, HD),
        new_keys.reshape(SEQS, STEPS, HD),
        new_values.reshape(SEQS, STEPS, HD),
        residual,
        out_weight,
        norm_gain.reshape(4, 128),
        gate_weight,
        up_weight,
        down_weight,
    )
    return pl.pallas_call(
        write_out,
        out_shape=(jax.ShapeDtypeStruct((KV, COLS), BF16), jax.ShapeDtypeStruct((4, COLS), BF16)),
        in_specs=[vmem, vmem],
        out_specs=(vmem, vmem),
    )(after, layer)


def solution(mesh):
    return jax.shard_map(
        local,
        mesh=mesh,
        in_specs=(
            P(None, None, "tp", None),
            P(None, "kv", "tp", None),
            P(None, "kv", "tp", None),
            P(None, None, "tp", None),
            P(None, None, "tp", None),
            P(),
            P(None, "kv"),
            P("tp", "kv"),
            P("kv"),
            P("kv", "tp"),
            P("kv", "tp"),
            P("tp", "kv"),
        ),
        out_specs=(P(None, "kv"), P("tp", "kv")),
        check_vma=False,
    )
```

```python
import math

import jax
import jax.numpy as jnp
from jax import lax
from jax.experimental import pallas as pl
from jax.experimental.pallas import tpu as pltpu
from jax.sharding import PartitionSpec as P

F32, BF16 = jnp.float32, jnp.bfloat16
MESH = pl.DeviceIdType.MESH
Z, Y, TP = 8, 4, 8
KV = Z * Y
SEQS, STEPS, HEADS, HD = 8, 4, 16, 128
CTX = 256
COLS = 512
MODEL = 16384
FF = 3328
FAR_FIRST = (4, 3, 5, 2, 6, 1, 7, 0)
HOPS = lambda o: min(o[0], Z - o[0]) + min(o[1], Y - o[1])
OTHERS = sorted(((d, e) for d in range(Z) for e in range(Y) if d or e), key=HOPS, reverse=True)


def slot_of(d, e):
    return (Z - d) % Z * Y + (Y - e) % Y - 1


SCALE = 1.0 / math.sqrt(HD)
LOW = -1e30


def drain(ref, sem):
    pltpu.make_async_copy(ref, ref, sem).wait()


def by_width(c, body):
    @pl.when(c < 6)
    def _():
        body(3)

    @pl.when(c >= 6)
    def _():
        body(4)


def start_of(c):
    return pl.multiple_of(c * 384 + jnp.maximum(c - 6, 0) * 128, 128)


def kernel(
    lengths_in,
    q_in, k_in, v_in, nk_in, nv_in, res_in, wo_in, gain_in, wg_in, wu_in, wd_in,
    after_out, layer_out,
    lengths, qv, kb, vb, nkb, nvb, resb, wo, gainb, wg, wu, wd,
    obuf, sbuf, ra, rs, tb, gb, gf, pr, aft,
    sq, yb, yr, own_sum, zs, zr, hr, hsent, down_sum, fs, fr,
    load_sem, a_send, a_recv, b_send, b_recv, c_send, c_recv,
    sq_send, sq_recv, y_send, y_recv, z_send, z_recv, h_send, h_recv, f_send, f_recv,
):
    kv, tp = lax.axis_index("kv"), lax.axis_index("tp")
    z, y = kv // Y, kv % Y
    x, core = tp // 2, tp % 2

    pairs = (
        (lengths_in, lengths), (q_in, qv), (k_in, kb), (v_in, vb), (nk_in, nkb), (nv_in, nvb), (res_in, resb), (gain_in, gainb),
        (wo_in, wo), (wg_in, wg), (wu_in, wu), (wd_in, wd),
    )
    loads = [pltpu.make_async_copy(a, b, load_sem.at[i]) for i, (a, b) in enumerate(pairs)]
    l_len, l_q, l_k, l_v, l_nk, l_nv, l_res, l_gain, l_wo, l_wg, l_wu, l_wd = loads

    def send(src, dst, send_sem, recv_sem, to):
        pltpu.make_async_remote_copy(
            src_ref=src, dst_ref=dst, send_sem=send_sem, recv_sem=recv_sem, device_id=to, device_id_type=MESH
        ).start()

    def of_plane(d, e):
        return lax.rem(z + d, Z) * Y + lax.rem(y + e, Y)

    for copy in loads[:4]:
        copy.start()
    barrier = pltpu.get_barrier_semaphore()

    @pl.loop(0, KV - 1)
    def _(i):
        j = i // Y
        d = 4 + j // 2 - j % 2 * (j // 2 * 2 + 1)
        pl.semaphore_signal(barrier, inc=1, device_id=(of_plane(d, (i + 1) % Y), tp), device_id_type=MESH)

    @pl.loop(1, TP)
    def _(i):
        pl.semaphore_signal(barrier, inc=1, device_id=(kv, lax.rem(tp + i, TP)), device_id_type=MESH)

    for copy in loads[4:]:
        copy.start()

    l_len.wait()
    l_q.wait()
    l_k.wait()
    l_v.wait()
    position = lax.broadcasted_iota(jnp.int32, (STEPS * HEADS, CTX), 1) + kv * CTX
    lane = lax.broadcasted_iota(jnp.int32, (128, 128), 1)
    stats = jnp.zeros((128, 128), F32)
    for s in range(SEQS):
        rows = qv[s * STEPS : (s + 1) * STEPS].reshape(STEPS * HEADS, HD)
        scores = lax.dot_general(rows, kb[s], (((1,), (1,)), ((), ())), preferred_element_type=F32) * SCALE
        inside = position < lengths[s]
        scores = jnp.where(inside, scores, LOW)
        top = jnp.max(scores, axis=1, keepdims=True)
        weights = jnp.where(inside, jnp.exp(scores - top), 0.0)
        total = jnp.sum(weights, axis=1, keepdims=True)
        sums = jnp.dot(weights.astype(BF16), vb[s], preferred_element_type=F32)
        obuf[s * STEPS : (s + 1) * STEPS] = sums.reshape(STEPS, HEADS, HD).astype(BF16)
        stats = jnp.where(lane == s, jnp.concatenate([top, total], axis=0), stats)
    turned = stats.T
    for s in range(SEQS):
        sbuf[s] = turned[s : s + 1]

    pl.semaphore_wait(barrier, KV - 1 + TP - 1)

    for d, e in OTHERS:
        to = of_plane(d, e)
        send(sbuf.at[to // Y], rs.at[slot_of(d, e)], a_send.at[0], a_recv.at[0], (to, tp))
        send(obuf.at[to], ra.at[slot_of(d, e)], a_send.at[1], a_recv.at[1], (to, tp))

    l_nk.wait()
    l_nv.wait()
    own_q = qv[kv].astype(F32)
    fresh_k, fresh_v = nkb[z].astype(F32), nvb[z].astype(F32)
    fresh = []
    for u in range(STEPS):
        score = jnp.sum(own_q * fresh_k[u : u + 1], axis=1, keepdims=True) * SCALE
        fresh.append(jnp.where(u <= y, score, LOW))
    rs[KV - 1] = sbuf[z]
    drain(rs.at[0 : KV - 1], a_recv.at[0])
    tb[:, 0:KV] = rs[...].reshape(KV, 128).T
    tops = tb[pl.ds(pl.multiple_of(y * HEADS, HEADS), HEADS), 0:KV]
    totals = tb[pl.ds(pl.multiple_of(64 + y * HEADS, HEADS), HEADS), 0:KV]
    row_max = jnp.max(tops, axis=1, keepdims=True)
    for score in fresh:
        row_max = jnp.maximum(row_max, score)
    factor = jnp.exp(tops - row_max)
    denominator = jnp.sum(factor * totals, axis=1, keepdims=True)
    numerator = factor[:, KV - 1 : KV] * obuf[kv].astype(F32)
    for u in range(STEPS):
        weight = jnp.where(u <= y, jnp.exp(fresh[u] - row_max), 0.0)
        denominator += weight
        numerator += weight.astype(BF16).astype(F32) * fresh_v[u : u + 1]
    drain(ra, a_recv.at[1])
    for j in range(KV - 1):
        numerator += factor[:, j : j + 1] * ra[j].astype(F32)
    gb[kv] = (numerator / denominator).astype(BF16)

    for d, e in OTHERS:
        send(gb.at[kv], gb.at[kv], b_send, b_recv, (of_plane(d, e), tp))

    l_wo.wait()
    l_res.wait()
    l_gain.wait()
    drain(gb.at[0 : KV - 1], b_recv)
    gf[...] = gb[...].astype(F32).reshape(KV * HEADS, HD)
    attended = jnp.concatenate(
        [gf[pl.ds(h, KV, stride=HEADS), :].astype(BF16) for h in range(HEADS)], axis=1
    )
    pr[tp] = jnp.dot(attended, wo[...], preferred_element_type=F32).astype(BF16)

    for i in FAR_FIRST[:-1]:
        send(pr.at[tp], pr.at[tp], c_send, c_recv, (kv, lax.rem(tp + i, TP)))

    drain(pr.at[0 : TP - 1], c_recv)
    summed = resb[...].astype(F32)
    for t in range(TP):
        summed += pr[t].astype(F32)
    after = summed.astype(BF16)
    wide = after.astype(F32)
    aft[...] = wide
    after_out[...] = after

    normed = jnp.concatenate(
        [wide[:, j * 128 : (j + 1) * 128] * gainb[j : j + 1].astype(F32) for j in range(COLS // 128)], axis=1
    ).astype(BF16)

    def send_squares():
        squares = jnp.broadcast_to(jnp.sum(wide * wide, axis=1, keepdims=True), (KV, 128)).T
        sq[KV - 1, :, 0:KV] = squares[0:1]
        for d, e in OTHERS:
            send(sq.at[KV - 1], sq.at[slot_of(d, e)], sq_send, sq_recv, (of_plane(d, e), tp))

    def multiply(d):
        c = lax.rem(z + d, Z)

        def body(n):
            block = pl.ds(start_of(c), n * 128)
            gate = jnp.dot(normed, wg[:, block], preferred_element_type=F32)
            up = jnp.dot(normed, wu[:, block], preferred_element_type=F32)
            for i in range(n):
                for half, value in enumerate((gate, up)):
                    tile = value[:, i * 128 : (i + 1) * 128].reshape(Y, 8, 128)
                    yb[d, :, :, i * 256 + half * 128 : i * 256 + half * 128 + 128] = tile.astype(BF16)
            for e in (2, 1, 3):
                send(
                    yb.at[d, lax.rem(y + e, Y), :, 0 : n * 256],
                    yr.at[d, Y - 1 - e, :, 0 : n * 256],
                    y_send.at[d],
                    y_recv.at[d],
                    (of_plane(0, e), tp),
                )

        by_width(c, body)

    l_wg.wait()
    l_wu.wait()
    for d in FAR_FIRST:
        multiply(d)
        if d == FAR_FIRST[1]:
            send_squares()

    def finish_y(d):
        c = lax.rem(z + d, Z)

        def body(n):
            n = n * 256
            drain(yr.at[d, :, :, 0:n], y_recv.at[d])
            part = yb[d, y, :, 0:n].astype(F32)
            for i in range(Y - 1):
                part += yr[d, i, :, 0:n].astype(F32)
            if d == 0:
                own_sum[:, 0:n] = part
            else:
                zs[d, :, 0:n] = part.astype(BF16)
                send(zs.at[d, :, 0:n], zr.at[Z - 1 - d, :, 0:n], z_send.at[d], z_recv, (of_plane(d, 0), tp))

        by_width(c, body)

    for d in FAR_FIRST:
        finish_y(d)

    drain(sq.at[0 : KV - 1], sq_recv)
    tb[...] = jnp.broadcast_to(jnp.sum(sq[...].reshape(KV, 128), axis=0, keepdims=True), (128, 128)).T
    inverse = lax.rsqrt(tb[pl.ds(pl.multiple_of(y * 8, 8), 8), :] / MODEL + 1e-05)

    by_width(z, lambda n: drain(zr.at[:, :, 0 : n * 256], z_recv))
    both = own_sum[...]
    for i in range(Z - 1):
        both += zr[i].astype(F32)
    for j in range(4):
        gate = both[:, j * 256 : j * 256 + 128] * inverse
        up = both[:, j * 256 + 128 : j * 256 + 256] * inverse
        hr[z, y, :, j * 128 : (j + 1) * 128] = (gate / (1.0 + jnp.exp(-gate)) * up).astype(BF16)

    def send_hidden(n):
        own = hr.at[z, y, :, 0 : n * 128]
        for d, e in OTHERS:
            send(own, own, h_send, h_recv.at[(Z - d) % Z], (of_plane(d, e), tp))

    by_width(z, send_hidden)

    def multiply_down(d):
        c = lax.rem(z + d, Z)

        def body(n):
            drain(hr.at[c, 0 : Y - (d == 0), :, 0 : n * 128], h_recv.at[d])
            hidden = hr[c, :, :, 0 : n * 128].astype(F32).reshape(KV, n * 128).astype(BF16)
            part = jnp.dot(hidden, wd[pl.ds(start_of(c), n * 128), :], preferred_element_type=F32)
            if d == 0:
                down_sum[...] = part
            else:
                down_sum[...] += part

        by_width(c, body)

    l_wd.wait()
    for d in FAR_FIRST[::-1]:
        multiply_down(d)
    down = down_sum[...]
    fs[...] = down.reshape(4, 8, COLS).astype(BF16)

    for i in FAR_FIRST[:-1]:
        to = lax.rem(tp + i, TP)
        send(fs.at[to // 2], fr.at[TP - 1 - i], f_send, f_recv, (kv, to))

    rows = aft[pl.ds(pl.multiple_of(x * 8, 8), 8), :] + fs[x].astype(F32)
    drain(fr, f_recv)
    for i in range(TP - 1):
        rows += fr[i].astype(F32)
    layer_out[...] = jnp.where(core == 0, rows[0:4], rows[4:8]).astype(BF16)

    drain(rs.at[0 : KV - 1], a_send.at[0])
    drain(ra, a_send.at[1])
    drain(gb.at[0 : KV - 1], b_send)
    drain(pr.at[0 : TP - 1], c_send)
    drain(sq.at[0 : KV - 1], sq_send)
    for d in range(Z):

        def left(n, d=d):
            drain(yr.at[d, :, :, 0 : n * 256], y_send.at[d])
            if d:
                drain(zs.at[d, :, 0 : n * 256], z_send.at[d])

        by_width(lax.rem(z + d, Z), left)
    by_width(z, lambda n: drain(hsent.at[:, :, 0 : n * 128], h_send))
    drain(fr, f_send)


def write_out(after_in, layer_in, after_out, layer_out, sem):
    copies = [
        pltpu.make_async_copy(after_in, after_out, sem.at[0]),
        pltpu.make_async_copy(layer_in, layer_out, sem.at[1]),
    ]
    for copy in copies:
        copy.start()
    for copy in copies:
        copy.wait()


def local(queries, cache_keys, cache_values, new_keys, new_values, lengths, residual, out_weight, norm_gain,
          gate_weight, up_weight, down_weight):
    hbm = pl.BlockSpec(memory_space=pl.ANY)
    vmem = pl.BlockSpec(memory_space=pltpu.VMEM)
    dma = pltpu.SemaphoreType.DMA
    after, layer = pl.pallas_call(
        kernel,
        out_shape=(pltpu.VMEM((KV, COLS), BF16), pltpu.VMEM((4, COLS), BF16)),
        in_specs=[hbm] * 12,
        out_specs=(vmem, vmem),
        scratch_shapes=[
            pltpu.SMEM((SEQS,), jnp.int32),
            pltpu.VMEM((KV, HEADS, HD), BF16),
            pltpu.VMEM((SEQS, CTX, HD), BF16),
            pltpu.VMEM((SEQS, CTX, HD), BF16),
            pltpu.VMEM((SEQS, STEPS, HD), BF16),
            pltpu.VMEM((SEQS, STEPS, HD), BF16),
            pltpu.VMEM((KV, COLS), BF16),
            pltpu.VMEM((HEADS * HD, COLS), BF16),
            pltpu.VMEM((4, 128), BF16),
            pltpu.VMEM((COLS, FF), BF16),
            pltpu.VMEM((COLS, FF), BF16),
            pltpu.VMEM((FF, COLS), BF16),
            pltpu.VMEM((KV, HEADS, HD), BF16),
            pltpu.VMEM((SEQS, 1, 128), F32),
            pltpu.VMEM((KV - 1, HEADS, HD), BF16),
            pltpu.VMEM((KV, 1, 128), F32),
            pltpu.VMEM((128, 128), F32),
            pltpu.VMEM((KV, HEADS, HD), BF16),
            pltpu.VMEM((KV * HEADS, HD), F32),
            pltpu.VMEM((TP, KV, COLS), BF16),
            pltpu.VMEM((KV, COLS), F32),
            pltpu.VMEM((KV, 1, 128), F32),
            pltpu.VMEM((Z, Y, 8, 1024), BF16),
            pltpu.VMEM((Z, Y - 1, 8, 1024), BF16),
            pltpu.VMEM((8, 1024), F32),
            pltpu.VMEM((Z, 8, 1024), BF16),
            pltpu.VMEM((Z - 1, 8, 1024), BF16),
            pltpu.VMEM((Z, Y, 8, 512), BF16),
            pltpu.VMEM((KV - 1, 8, 512), BF16),
            pltpu.VMEM((KV, COLS), F32),
            pltpu.VMEM((4, 8, COLS), BF16),
            pltpu.VMEM((TP - 1, 8, COLS), BF16),
            dma((12,)), dma((2,)), dma((2,)), dma, dma, dma, dma,
            dma, dma, dma((Z,)), dma((Z,)), dma((Z,)), dma, dma, dma((Z,)), dma, dma,
        ],
        compiler_params=pltpu.CompilerParams(
            collective_id=0, has_side_effects=True, vmem_limit_bytes=60 * 1024 * 1024
        ),
    )(
        *(
            pltpu.with_memory_space_constraint(array, pltpu.HBM)
            for array in (
                lengths,
                queries.reshape(KV, HEADS, HD),
                cache_keys.reshape(SEQS, CTX, HD),
                cache_values.reshape(SEQS, CTX, HD),
                new_keys.reshape(SEQS, STEPS, HD),
                new_values.reshape(SEQS, STEPS, HD),
                residual,
                out_weight,
                norm_gain.reshape(4, 128),
                gate_weight,
                up_weight,
                down_weight,
            )
        )
    )
    return pl.pallas_call(
        write_out,
        out_shape=(jax.ShapeDtypeStruct((KV, COLS), BF16), jax.ShapeDtypeStruct((4, COLS), BF16)),
        in_specs=[vmem, vmem],
        out_specs=(hbm, hbm),
        scratch_shapes=[dma((2,))],
        compiler_params=pltpu.CompilerParams(vmem_limit_bytes=1024 * 1024),
    )(after, layer)


def solution(mesh):
    return jax.shard_map(
        local,
        mesh=mesh,
        in_specs=(
            P(None, None, "tp", None),
            P(None, "kv", "tp", None),
            P(None, "kv", "tp", None),
            P(None, None, "tp", None),
            P(None, None, "tp", None),
            P(),
            P(None, "kv"),
            P("tp", "kv"),
            P("kv"),
            P("kv", "tp"),
            P("kv", "tp"),
            P("tp", "kv"),
        ),
        out_specs=(P(None, "kv"), P("tp", "kv")),
        check_vma=False,
    )
```

```python
import math

import jax
import jax.numpy as jnp
from jax import lax
from jax.experimental import pallas as pl
from jax.experimental.pallas import tpu as pltpu
from jax.sharding import PartitionSpec as P

F32, BF16 = jnp.float32, jnp.bfloat16
MESH = pl.DeviceIdType.MESH
Z, Y, TP = 8, 4, 8
KV = Z * Y
SEQS, STEPS, HEADS, HD = 8, 4, 16, 128
CTX = 256
COLS = 512
MODEL = 16384
FF = 3328
WIDTH = (3, 3, 3, 3, 3, 3, 4, 4)
FAR_FIRST = (4, 3, 5, 2, 6, 1, 7, 0)
NEAR = (1, 7)
HOPS = lambda o: min(o[0], Z - o[0]) + min(o[1], Y - o[1])
OTHERS = sorted(((d, e) for d in range(Z) for e in range(Y) if d or e), key=HOPS, reverse=True)


def slot_of(d, e):
    return (Z - d) % Z * Y + (Y - e) % Y - 1


SCALE = 1.0 / math.sqrt(HD)
LOW = -1e30


def drain(ref, sem):
    pltpu.make_async_copy(ref, ref, sem).wait()


def by_width(c, body):
    @pl.when(c < 6)
    def _():
        body(3)

    @pl.when(c >= 6)
    def _():
        body(4)


def start_of(c):
    return pl.multiple_of(c * 384 + jnp.maximum(c - 6, 0) * 128, 128)


def kernel(
    lengths_in,
    q_in, k_in, v_in, nk_in, nv_in, res_in, wo_in, gain_in, wg_in, wu_in, wd_in,
    after_out, layer_out,
    lengths, qv, kb, vb, nkb, nvb, resb, wo, gainb, wg, wu, wd,
    obuf, sbuf, ra, rs, tb, gb, gf, pr, aft,
    sq, yb, yr, own_part, own_sum, nr, zs, zr, hr, hsent, fs, fr,
    load_sem, a_send, a_recv, b_send, b_recv, c_send, c_recv,
    sq_send, sq_recv, y_send, y_recv, n_recv, z_send, z_recv, h_send, h_recv, f_send, f_recv,
):
    kv, tp = lax.axis_index("kv"), lax.axis_index("tp")
    z, y = kv // Y, kv % Y
    x, core = tp // 2, tp % 2

    pairs = (
        (lengths_in, lengths), (q_in, qv), (k_in, kb), (v_in, vb), (nk_in, nkb), (nv_in, nvb), (res_in, resb), (gain_in, gainb),
        (wo_in, wo), (wg_in, wg), (wu_in, wu), (wd_in, wd),
    )
    loads = [pltpu.make_async_copy(a, b, load_sem.at[i]) for i, (a, b) in enumerate(pairs)]
    l_len, l_q, l_k, l_v, l_nk, l_nv, l_res, l_gain, l_wo, l_wg, l_wu, l_wd = loads

    def send(src, dst, send_sem, recv_sem, to):
        pltpu.make_async_remote_copy(
            src_ref=src, dst_ref=dst, send_sem=send_sem, recv_sem=recv_sem, device_id=to, device_id_type=MESH
        ).start()

    def of_plane(d, e):
        return lax.rem(z + d, Z) * Y + lax.rem(y + e, Y)

    for copy in loads[:4]:
        copy.start()
    barrier = pltpu.get_barrier_semaphore()

    @pl.loop(0, KV - 1)
    def _(i):
        j = i // Y
        d = 4 + j // 2 - j % 2 * (j // 2 * 2 + 1)
        pl.semaphore_signal(barrier, inc=1, device_id=(of_plane(d, (i + 1) % Y), tp), device_id_type=MESH)

    @pl.loop(1, TP)
    def _(i):
        pl.semaphore_signal(barrier, inc=1, device_id=(kv, lax.rem(tp + i, TP)), device_id_type=MESH)

    for copy in loads[4:]:
        copy.start()

    l_len.wait()
    l_q.wait()
    l_k.wait()
    l_v.wait()
    position = lax.broadcasted_iota(jnp.int32, (STEPS * HEADS, CTX), 1) + kv * CTX
    lane = lax.broadcasted_iota(jnp.int32, (128, 128), 1)
    stats = jnp.zeros((128, 128), F32)
    for s in range(SEQS):
        rows = qv[s * STEPS : (s + 1) * STEPS].reshape(STEPS * HEADS, HD)
        scores = lax.dot_general(rows, kb[s], (((1,), (1,)), ((), ())), preferred_element_type=F32) * SCALE
        inside = position < lengths[s]
        scores = jnp.where(inside, scores, LOW)
        top = jnp.max(scores, axis=1, keepdims=True)
        weights = jnp.where(inside, jnp.exp(scores - top), 0.0)
        total = jnp.sum(weights, axis=1, keepdims=True)
        sums = jnp.dot(weights.astype(BF16), vb[s], preferred_element_type=F32)
        obuf[s * STEPS : (s + 1) * STEPS] = sums.reshape(STEPS, HEADS, HD).astype(BF16)
        stats = jnp.where(lane == s, jnp.concatenate([top, total], axis=0), stats)
    turned = stats.T
    for s in range(SEQS):
        sbuf[s] = turned[s : s + 1]

    pl.semaphore_wait(barrier, KV - 1 + TP - 1)

    for d, e in OTHERS:
        to = of_plane(d, e)
        send(sbuf.at[to // Y], rs.at[slot_of(d, e)], a_send.at[0], a_recv.at[0], (to, tp))
        send(obuf.at[to], ra.at[slot_of(d, e)], a_send.at[1], a_recv.at[1], (to, tp))

    l_nk.wait()
    l_nv.wait()
    own_q = qv[kv].astype(F32)
    fresh_k, fresh_v = nkb[z].astype(F32), nvb[z].astype(F32)
    fresh = []
    for u in range(STEPS):
        score = jnp.sum(own_q * fresh_k[u : u + 1], axis=1, keepdims=True) * SCALE
        fresh.append(jnp.where(u <= y, score, LOW))
    rs[KV - 1] = sbuf[z]
    drain(rs.at[0 : KV - 1], a_recv.at[0])
    tb[:, 0:KV] = rs[...].reshape(KV, 128).T
    tops = tb[pl.ds(pl.multiple_of(y * HEADS, HEADS), HEADS), 0:KV]
    totals = tb[pl.ds(pl.multiple_of(64 + y * HEADS, HEADS), HEADS), 0:KV]
    row_max = jnp.max(tops, axis=1, keepdims=True)
    for score in fresh:
        row_max = jnp.maximum(row_max, score)
    factor = jnp.exp(tops - row_max)
    denominator = jnp.sum(factor * totals, axis=1, keepdims=True)
    numerator = factor[:, KV - 1 : KV] * obuf[kv].astype(F32)
    for u in range(STEPS):
        weight = jnp.where(u <= y, jnp.exp(fresh[u] - row_max), 0.0)
        denominator += weight
        numerator += weight.astype(BF16).astype(F32) * fresh_v[u : u + 1]
    drain(ra, a_recv.at[1])
    for j in range(KV - 1):
        numerator += factor[:, j : j + 1] * ra[j].astype(F32)
    gb[kv] = (numerator / denominator).astype(BF16)

    for d, e in OTHERS:
        send(gb.at[kv], gb.at[kv], b_send, b_recv, (of_plane(d, e), tp))

    l_wo.wait()
    l_res.wait()
    l_gain.wait()
    drain(gb.at[0 : KV - 1], b_recv)
    gf[...] = gb[...].astype(F32).reshape(KV * HEADS, HD)
    attended = jnp.concatenate(
        [gf[pl.ds(h, KV, stride=HEADS), :].astype(BF16) for h in range(HEADS)], axis=1
    )
    pr[tp] = jnp.dot(attended, wo[...], preferred_element_type=F32).astype(BF16)
    for i in FAR_FIRST[:-1]:
        send(pr.at[tp], pr.at[tp], c_send, c_recv, (kv, lax.rem(tp + i, TP)))

    drain(pr.at[0 : TP - 1], c_recv)
    summed = resb[...].astype(F32)
    for t in range(TP):
        summed += pr[t].astype(F32)
    after = summed.astype(BF16)
    wide = after.astype(F32)
    aft[...] = wide
    after_out[...] = after

    normed = jnp.concatenate(
        [wide[:, j * 128 : (j + 1) * 128] * gainb[j : j + 1].astype(F32) for j in range(COLS // 128)], axis=1
    ).astype(BF16)

    def send_squares():
        squares = jnp.broadcast_to(jnp.sum(wide * wide, axis=1, keepdims=True), (KV, 128)).T
        sq[KV - 1, :, 0:KV] = squares[0:1]
        for d, e in OTHERS:
            send(sq.at[KV - 1], sq.at[slot_of(d, e)], sq_send, sq_recv, (of_plane(d, e), tp))

    def send_y(d, n):
        for e in (2, 1, 3):
            send(
                yb.at[d, lax.rem(y + e, Y), :, 0 : n * 256],
                yr.at[d, Y - 1 - e, :, 0 : n * 256],
                y_send.at[d],
                y_recv.at[d],
                (of_plane(0, e), tp),
            )

    def add_near(n):
        for i in range(2):
            drain(nr.at[i, :, :, 0 : n * 256], n_recv.at[i])
        part = own_part[:, :, 0 : n * 256] + nr[0, :, :, 0 : n * 256].astype(F32) + nr[1, :, :, 0 : n * 256].astype(F32)
        own_part[:, :, 0 : n * 256] = part
        yb[0, :, :, 0 : n * 256] = part.astype(BF16)
        send_y(0, n)

    def multiply(d):
        c = lax.rem(z + d, Z)

        def body(n):
            block = pl.ds(start_of(c), n * 128)
            gate = jnp.dot(normed, wg[:, block], preferred_element_type=F32)
            up = jnp.dot(normed, wu[:, block], preferred_element_type=F32)
            for i in range(n):
                for half, value in enumerate((gate, up)):
                    tile = value[:, i * 128 : (i + 1) * 128].reshape(Y, 8, 128)
                    at = i * 256 + half * 128
                    if d == 0:
                        own_part[:, :, at : at + 128] = tile
                    else:
                        yb[d, :, :, at : at + 128] = tile.astype(BF16)
            if d in NEAR:
                send(
                    yb.at[d, :, :, 0 : n * 256],
                    nr.at[NEAR.index(d), :, :, 0 : n * 256],
                    y_send.at[d],
                    n_recv.at[NEAR.index(d)],
                    (of_plane(d, 0), tp),
                )
            elif d:
                send_y(d, n)

        by_width(c, body)

    l_wg.wait()
    l_wu.wait()
    for d in FAR_FIRST:
        multiply(d)
        if d == FAR_FIRST[1]:
            send_squares()

    def finish_y(d):
        c = lax.rem(z + d, Z)

        def body(n):
            n = n * 256
            drain(yr.at[d, :, :, 0:n], y_recv.at[d])
            part = yb[d, y, :, 0:n].astype(F32) if d else own_part[y, :, 0:n]
            for i in range(Y - 1):
                part += yr[d, i, :, 0:n].astype(F32)
            if d == 0:
                own_sum[:, 0:n] = part
            else:
                zs[d, :, 0:n] = part.astype(BF16)
                send(zs.at[d, :, 0:n], zr.at[6 - d, :, 0:n], z_send.at[d], z_recv, (of_plane(d, 0), tp))

        by_width(c, body)

    for d in (4, 3, 5):
        finish_y(d)
    by_width(z, add_near)
    for d in (2, 6, 0):
        finish_y(d)

    drain(sq.at[0 : KV - 1], sq_recv)
    tb[...] = jnp.broadcast_to(jnp.sum(sq[...].reshape(KV, 128), axis=0, keepdims=True), (128, 128)).T
    inverse = lax.rsqrt(tb[pl.ds(pl.multiple_of(y * 8, 8), 8), :] / MODEL + 1e-05)

    by_width(z, lambda n: drain(zr.at[:, :, 0 : n * 256], z_recv))
    both = own_sum[...]
    for i in range(Z - 3):
        both += zr[i].astype(F32)
    for j in range(4):
        gate = both[:, j * 256 : j * 256 + 128] * inverse
        up = both[:, j * 256 + 128 : j * 256 + 256] * inverse
        hr[z, y, :, j * 128 : (j + 1) * 128] = (gate / (1.0 + jnp.exp(-gate)) * up).astype(BF16)

    def send_hidden(n):
        own = hr.at[z, y, :, 0 : n * 128]
        for d, e in OTHERS:
            send(own, own, h_send, h_recv.at[(Z - d) % Z], (of_plane(d, e), tp))

    by_width(z, send_hidden)

    l_wd.wait()
    for d in (0, 4, 3, 5, 2, 6, 1, 7):
        c = lax.rem(z + d, Z)
        by_width(c, lambda n, c=c, d=d: drain(hr.at[c, 0 : Y - (d == 0), :, 0 : n * 128], h_recv.at[d]))
    hidden = jnp.concatenate(
        [hr[c, :, :, 0 : WIDTH[c] * 128].astype(F32).reshape(KV, WIDTH[c] * 128).astype(BF16) for c in range(Z)], axis=1
    )
    down = jnp.dot(hidden, wd[...], preferred_element_type=F32)
    fs[...] = down.reshape(4, 8, COLS).astype(BF16)

    for i in FAR_FIRST[:-1]:
        to = lax.rem(tp + i, TP)
        send(fs.at[to // 2], fr.at[TP - 1 - i], f_send, f_recv, (kv, to))

    rows = aft[pl.ds(pl.multiple_of(x * 8, 8), 8), :] + fs[x].astype(F32)
    drain(fr, f_recv)
    for i in range(TP - 1):
        rows += fr[i].astype(F32)
    layer_out[...] = jnp.where(core == 0, rows[0:4], rows[4:8]).astype(BF16)

    drain(rs.at[0 : KV - 1], a_send.at[0])
    drain(ra, a_send.at[1])
    drain(gb.at[0 : KV - 1], b_send)
    drain(pr.at[0 : TP - 1], c_send)
    drain(sq.at[0 : KV - 1], sq_send)
    for d in range(Z):

        def left(n, d=d):
            drain(yb.at[d, 0 : Y - (d not in NEAR), :, 0 : n * 256], y_send.at[d])
            if d and d not in NEAR:
                drain(zs.at[d, :, 0 : n * 256], z_send.at[d])

        by_width(lax.rem(z + d, Z), left)
    by_width(z, lambda n: drain(hsent.at[:, :, 0 : n * 128], h_send))
    drain(fr, f_send)


def write_out(after_in, layer_in, after_out, layer_out, sem):
    copies = [
        pltpu.make_async_copy(after_in, after_out, sem.at[0]),
        pltpu.make_async_copy(layer_in, layer_out, sem.at[1]),
    ]
    for copy in copies:
        copy.start()
    for copy in copies:
        copy.wait()


def local(queries, cache_keys, cache_values, new_keys, new_values, lengths, residual, out_weight, norm_gain,
          gate_weight, up_weight, down_weight):
    hbm = pl.BlockSpec(memory_space=pl.ANY)
    vmem = pl.BlockSpec(memory_space=pltpu.VMEM)
    dma = pltpu.SemaphoreType.DMA
    after, layer = pl.pallas_call(
        kernel,
        out_shape=(pltpu.VMEM((KV, COLS), BF16), pltpu.VMEM((4, COLS), BF16)),
        in_specs=[hbm] * 12,
        out_specs=(vmem, vmem),
        scratch_shapes=[
            pltpu.SMEM((SEQS,), jnp.int32),
            pltpu.VMEM((KV, HEADS, HD), BF16),
            pltpu.VMEM((SEQS, CTX, HD), BF16),
            pltpu.VMEM((SEQS, CTX, HD), BF16),
            pltpu.VMEM((SEQS, STEPS, HD), BF16),
            pltpu.VMEM((SEQS, STEPS, HD), BF16),
            pltpu.VMEM((KV, COLS), BF16),
            pltpu.VMEM((HEADS * HD, COLS), BF16),
            pltpu.VMEM((4, 128), BF16),
            pltpu.VMEM((COLS, FF), BF16),
            pltpu.VMEM((COLS, FF), BF16),
            pltpu.VMEM((FF, COLS), BF16),
            pltpu.VMEM((KV, HEADS, HD), BF16),
            pltpu.VMEM((SEQS, 1, 128), F32),
            pltpu.VMEM((KV - 1, HEADS, HD), BF16),
            pltpu.VMEM((KV, 1, 128), F32),
            pltpu.VMEM((128, 128), F32),
            pltpu.VMEM((KV, HEADS, HD), BF16),
            pltpu.VMEM((KV * HEADS, HD), F32),
            pltpu.VMEM((TP, KV, COLS), BF16),
            pltpu.VMEM((KV, COLS), F32),
            pltpu.VMEM((KV, 1, 128), F32),
            pltpu.VMEM((Z, Y, 8, 1024), BF16),
            pltpu.VMEM((Z, Y - 1, 8, 1024), BF16),
            pltpu.VMEM((Y, 8, 1024), F32),
            pltpu.VMEM((8, 1024), F32),
            pltpu.VMEM((2, Y, 8, 1024), BF16),
            pltpu.VMEM((Z, 8, 1024), BF16),
            pltpu.VMEM((Z - 3, 8, 1024), BF16),
            pltpu.VMEM((Z, Y, 8, 512), BF16),
            pltpu.VMEM((KV - 1, 8, 512), BF16),
            pltpu.VMEM((4, 8, COLS), BF16),
            pltpu.VMEM((TP - 1, 8, COLS), BF16),
            dma((12,)), dma((2,)), dma((2,)), dma, dma, dma, dma,
            dma, dma, dma((Z,)), dma((Z,)), dma((2,)), dma((Z,)), dma, dma, dma((Z,)), dma, dma,
        ],
        compiler_params=pltpu.CompilerParams(
            collective_id=0, has_side_effects=True, vmem_limit_bytes=60 * 1024 * 1024
        ),
    )(
        *(
            pltpu.with_memory_space_constraint(array, pltpu.HBM)
            for array in (
                lengths,
                queries.reshape(KV, HEADS, HD),
                cache_keys.reshape(SEQS, CTX, HD),
                cache_values.reshape(SEQS, CTX, HD),
                new_keys.reshape(SEQS, STEPS, HD),
                new_values.reshape(SEQS, STEPS, HD),
                residual,
                out_weight,
                norm_gain.reshape(4, 128),
                gate_weight,
                up_weight,
                down_weight,
            )
        )
    )
    return pl.pallas_call(
        write_out,
        out_shape=(jax.ShapeDtypeStruct((KV, COLS), BF16), jax.ShapeDtypeStruct((4, COLS), BF16)),
        in_specs=[vmem, vmem],
        out_specs=(hbm, hbm),
        scratch_shapes=[dma((2,))],
        compiler_params=pltpu.CompilerParams(vmem_limit_bytes=1024 * 1024),
    )(after, layer)


def solution(mesh):
    return jax.shard_map(
        local,
        mesh=mesh,
        in_specs=(
            P(None, None, "tp", None),
            P(None, "kv", "tp", None),
            P(None, "kv", "tp", None),
            P(None, None, "tp", None),
            P(None, None, "tp", None),
            P(),
            P(None, "kv"),
            P("tp", "kv"),
            P("kv"),
            P("kv", "tp"),
            P("kv", "tp"),
            P("tp", "kv"),
        ),
        out_specs=(P(None, "kv"), P("tp", "kv")),
        check_vma=False,
    )
```

```python
import math

import jax
import jax.numpy as jnp
from jax import lax
from jax.experimental import pallas as pl
from jax.experimental.pallas import tpu as pltpu
from jax.sharding import PartitionSpec as P

F32, BF16 = jnp.float32, jnp.bfloat16
MESH = pl.DeviceIdType.MESH
Z, Y, TP = 8, 4, 8
KV = Z * Y
SEQS, STEPS, HEADS, HD = 8, 4, 16, 128
CTX = 256
COLS = 512
MODEL = 16384
FF = 3328
WIDTH = (3, 3, 3, 3, 3, 3, 4, 4)
FAR_FIRST = (4, 3, 5, 2, 6, 1, 7, 0)
NEAR = (1, 7)
Y_STAGE = (4, 3, 5, 2, 6, 0)
HOPS = lambda o: min(o[0], Z - o[0]) + min(o[1], Y - o[1])
OTHERS = sorted(((d, e) for d in range(Z) for e in range(Y) if d or e), key=HOPS, reverse=True)


def slot_of(d, e):
    return (Z - d) % Z * Y + (Y - e) % Y - 1


SCALE = 1.0 / math.sqrt(HD)
LOW = -1e30


def drain(ref, sem):
    pltpu.make_async_copy(ref, ref, sem).wait()


def by_width(c, body):
    @pl.when(c < 6)
    def _():
        body(3)

    @pl.when(c >= 6)
    def _():
        body(4)


def kernel(
    lengths_in,
    q_in, k_in, v_in, nk_in, nv_in, res_in, wo_in, gain_in, wg_in, wu_in, wd_in,
    after_out, layer_out,
    lengths, qv, kb, vb, nkb, nvb, resb, wo, gainb, wgu, wd,
    obuf, sbuf, ra, rs, tb, gb, gf, pr, aft,
    sq, yb, yr, own_part, own_sum, nr, zs, zr, hr, sized, fs, fr,
    load_sem, gu_sem, sent, a_recv, b_recv, c_recv, sq_recv, y_recv, n_recv, z_recv, h_recv, f_recv,
):
    kv, tp = lax.axis_index("kv"), lax.axis_index("tp")
    z, y = kv // Y, kv % Y
    x, core = tp // 2, tp % 2

    pairs = (
        (lengths_in, lengths), (q_in, qv), (k_in, kb), (v_in, vb), (nk_in, nkb), (nv_in, nvb), (res_in, resb), (gain_in, gainb),
        (wo_in, wo), (wd_in, wd),
    )
    loads = [pltpu.make_async_copy(a, b, load_sem.at[i]) for i, (a, b) in zip((0, 1, 1, 1, 2, 2, 3, 4, 5, 6), pairs)]

    def send(src, dst, send_sem, recv_sem, to):
        pltpu.make_async_remote_copy(
            src_ref=src, dst_ref=dst, send_sem=send_sem, recv_sem=recv_sem, device_id=to, device_id_type=MESH
        ).start()

    def of_plane(d, e):
        return lax.rem(z + d, Z) * Y + lax.rem(y + e, Y)

    for copy in loads[:4]:
        copy.start()
    barrier = pltpu.get_barrier_semaphore()

    @pl.loop(0, KV - 1)
    def _(i):
        j = i // Y
        d = 4 + j // 2 - j % 2 * (j // 2 * 2 + 1)
        pl.semaphore_signal(barrier, inc=1, device_id=(of_plane(d, (i + 1) % Y), tp), device_id_type=MESH)

    @pl.loop(1, TP)
    def _(i):
        pl.semaphore_signal(barrier, inc=1, device_id=(kv, lax.rem(tp + i, TP)), device_id_type=MESH)

    for copy in loads[4:]:
        copy.start()

    loads[0].wait()
    drain(wgu.at[:, 0:1152], load_sem.at[1])
    position = lax.broadcasted_iota(jnp.int32, (STEPS * HEADS, CTX), 1) + kv * CTX
    lane = lax.broadcasted_iota(jnp.int32, (128, 128), 1)
    stats = jnp.zeros((128, 128), F32)
    for s in range(SEQS):
        rows = qv[s * STEPS : (s + 1) * STEPS].reshape(STEPS * HEADS, HD)
        scores = lax.dot_general(rows, kb[s], (((1,), (1,)), ((), ())), preferred_element_type=F32) * SCALE
        inside = position < lengths[s]
        scores = jnp.where(inside, scores, LOW)
        top = jnp.max(scores, axis=1, keepdims=True)
        weights = jnp.where(inside, jnp.exp(scores - top), 0.0)
        total = jnp.sum(weights, axis=1, keepdims=True)
        sums = jnp.dot(weights.astype(BF16), vb[s], preferred_element_type=F32)
        obuf[s * STEPS : (s + 1) * STEPS] = sums.reshape(STEPS, HEADS, HD).astype(BF16)
        stats = jnp.where(lane == s, jnp.concatenate([top, total], axis=0), stats)
    turned = stats.T
    for s in range(SEQS):
        sbuf[s] = turned[s : s + 1]

    pl.semaphore_wait(barrier, KV - 1 + TP - 1)

    for d, e in OTHERS:
        to = of_plane(d, e)
        send(sbuf.at[to // Y], rs.at[slot_of(d, e)], sent, a_recv.at[0], (to, tp))
        send(obuf.at[to], ra.at[slot_of(d, e)], sent, a_recv.at[1], (to, tp))

    @pl.loop(0, FF // 128)
    def _(j):
        block = pl.ds(pl.multiple_of(j * 128, 128), 128)
        for half, weight in enumerate((wg_in, wu_in)):
            there = pl.ds(pl.multiple_of(j * 256 + half * 128, 128), 128)
            pltpu.make_async_copy(weight.at[:, block], wgu.at[:, there], gu_sem).start()

    drain(qv.at[0:4], load_sem.at[2])
    for copy in loads[6:]:
        copy.wait()
    own_q = qv[kv].astype(F32)
    fresh_k, fresh_v = nkb[z].astype(F32), nvb[z].astype(F32)
    fresh = []
    for u in range(STEPS):
        score = jnp.sum(own_q * fresh_k[u : u + 1], axis=1, keepdims=True) * SCALE
        fresh.append(jnp.where(u <= y, score, LOW))
    rs[KV - 1] = sbuf[z]
    drain(rs.at[0 : KV - 1], a_recv.at[0])
    drain(ra, a_recv.at[1])
    tb[:, 0:KV] = rs[...].reshape(KV, 128).T
    tops = tb[pl.ds(pl.multiple_of(y * HEADS, HEADS), HEADS), 0:KV]
    totals = tb[pl.ds(pl.multiple_of(64 + y * HEADS, HEADS), HEADS), 0:KV]
    row_max = jnp.max(tops, axis=1, keepdims=True)
    for score in fresh:
        row_max = jnp.maximum(row_max, score)
    factor = jnp.exp(tops - row_max)
    denominator = jnp.sum(factor * totals, axis=1, keepdims=True)
    numerator = factor[:, KV - 1 : KV] * obuf[kv].astype(F32)
    for u in range(STEPS):
        weight = jnp.where(u <= y, jnp.exp(fresh[u] - row_max), 0.0)
        denominator += weight
        numerator += weight.astype(BF16).astype(F32) * fresh_v[u : u + 1]
    for j in range(KV - 1):
        numerator += factor[:, j : j + 1] * ra[j].astype(F32)
    gb[kv] = (numerator / denominator).astype(BF16)

    for d, e in OTHERS:
        send(gb.at[kv], gb.at[kv], sent, b_recv, (of_plane(d, e), tp))

    drain(gb.at[0 : KV - 1], b_recv)
    gf[...] = gb[...].astype(F32).reshape(KV * HEADS, HD)
    attended = jnp.concatenate(
        [gf[pl.ds(h, KV, stride=HEADS), :].astype(BF16) for h in range(HEADS)], axis=1
    )
    pr[tp] = jnp.dot(attended, wo[...], preferred_element_type=F32).astype(BF16)
    for i in FAR_FIRST[:-1]:
        send(pr.at[tp], pr.at[tp], sent, c_recv, (kv, lax.rem(tp + i, TP)))

    drain(pr.at[0 : TP - 1], c_recv)
    summed = resb[...].astype(F32)
    for t in range(TP):
        summed += pr[t].astype(F32)
    after = summed.astype(BF16)
    wide = after.astype(F32)
    aft[...] = wide
    after_out[...] = after

    normed = jnp.concatenate(
        [wide[:, j * 128 : (j + 1) * 128] * gainb[j : j + 1].astype(F32) for j in range(COLS // 128)], axis=1
    ).astype(BF16)

    def send_squares():
        squares = jnp.broadcast_to(jnp.sum(wide * wide, axis=1, keepdims=True), (KV, 128)).T
        sq[KV - 1, :, 0:KV] = squares[0:1]
        for d, e in OTHERS:
            send(sq.at[KV - 1], sq.at[slot_of(d, e)], sent, sq_recv, (of_plane(d, e), tp))

    def send_y(d, n):
        for e in (2, 1, 3):
            send(
                yb.at[d, lax.rem(y + e, Y), :, 0 : n * 256],
                yr.at[d, Y - 1 - e, :, 0 : n * 256],
                sent,
                y_recv.at[Y_STAGE.index(d)],
                (of_plane(0, e), tp),
            )

    def add_near(n):
        drain(nr.at[:, :, :, 0 : n * 256], n_recv)
        part = own_part[:, :, 0 : n * 256] + nr[0, :, :, 0 : n * 256].astype(F32) + nr[1, :, :, 0 : n * 256].astype(F32)
        own_part[:, :, 0 : n * 256] = part
        yb[0, :, :, 0 : n * 256] = part.astype(BF16)
        send_y(0, n)

    def multiply(d):
        c = lax.rem(z + d, Z)

        def body(n):
            block = pl.ds(pl.multiple_of(c * 768 + jnp.maximum(c - 6, 0) * 256, 256), n * 256)
            both = jnp.dot(normed, wgu[:, block], preferred_element_type=F32).reshape(Y, 8, n * 256)
            if d == 0:
                own_part[:, :, 0 : n * 256] = both
            else:
                yb[d, :, :, 0 : n * 256] = both.astype(BF16)
            if d in NEAR:
                send(
                    yb.at[d, :, :, 0 : n * 256],
                    nr.at[NEAR.index(d), :, :, 0 : n * 256],
                    sent,
                    n_recv,
                    (of_plane(d, 0), tp),
                )
            elif d:
                send_y(d, n)

        by_width(c, body)

    drain(wgu, gu_sem)
    for d in (4, 3, 5, 1, 7, 2, 6, 0):
        multiply(d)
        if d == 6:
            send_squares()

    def finish_y(d):
        c = lax.rem(z + d, Z)

        def body(n):
            n = n * 256
            drain(yr.at[d, :, :, 0:n], y_recv.at[Y_STAGE.index(d)])
            part = yb[d, y, :, 0:n].astype(F32) if d else own_part[y, :, 0:n]
            for i in range(Y - 1):
                part += yr[d, i, :, 0:n].astype(F32)
            if d == 0:
                own_sum[:, 0:n] = part
            else:
                zs[d, :, 0:n] = part.astype(BF16)
                send(zs.at[d, :, 0:n], zr.at[6 - d, :, 0:n], sent, z_recv, (of_plane(d, 0), tp))

        by_width(c, body)

    for d in (4, 3, 5):
        finish_y(d)
    by_width(z, add_near)
    for d in (2, 6, 0):
        finish_y(d)

    drain(sq.at[0 : KV - 1], sq_recv)
    tb[...] = jnp.broadcast_to(jnp.sum(sq[...].reshape(KV, 128), axis=0, keepdims=True), (128, 128)).T
    inverse = lax.rsqrt(tb[pl.ds(pl.multiple_of(y * 8, 8), 8), :] / MODEL + 1e-05)

    by_width(z, lambda n: drain(zr.at[:, :, 0 : n * 256], z_recv))
    both = own_sum[...]
    for i in range(Z - 3):
        both += zr[i].astype(F32)
    for j in range(4):
        gate = both[:, j * 256 : j * 256 + 128] * inverse
        up = both[:, j * 256 + 128 : j * 256 + 256] * inverse
        hr[z, y, :, j * 128 : (j + 1) * 128] = (gate / (1.0 + jnp.exp(-gate)) * up).astype(BF16)

    def send_hidden(n):
        own = hr.at[z, y, :, 0 : n * 128]
        for d, e in OTHERS:
            send(own, own, sent, h_recv, (of_plane(d, e), tp))

    by_width(z, send_hidden)

    by_width(z, lambda n: drain(sized.at[0 : (Y * sum(WIDTH) - n) * 4], h_recv))
    hidden = jnp.concatenate(
        [hr[c, :, :, 0 : WIDTH[c] * 128].astype(F32).reshape(KV, WIDTH[c] * 128).astype(BF16) for c in range(Z)], axis=1
    )
    down = jnp.dot(hidden, wd[...], preferred_element_type=F32)
    fs[...] = down.reshape(4, 8, COLS).astype(BF16)

    for i in FAR_FIRST[:-1]:
        to = lax.rem(tp + i, TP)
        send(fs.at[to // 2], fr.at[TP - 1 - i], sent, f_recv, (kv, to))

    rows = aft[pl.ds(pl.multiple_of(x * 8, 8), 8), :] + fs[x].astype(F32)
    drain(fr, f_recv)
    for i in range(TP - 1):
        rows += fr[i].astype(F32)
    layer_out[...] = jnp.where(core == 0, rows[0:4], rows[4:8]).astype(BF16)

    def left(n):
        units = (KV - 1) * (1 + 8 + 8 + 1 + 4 * n) + (TP - 1) * (64 + 16) + (Y * sum(WIDTH) - n) * 8
        drain(sized.at[0:units], sent)

    by_width(z, left)


def write_out(after_in, layer_in, after_out, layer_out, sem):
    copies = [
        pltpu.make_async_copy(after_in, after_out, sem.at[0]),
        pltpu.make_async_copy(layer_in, layer_out, sem.at[1]),
    ]
    for copy in copies:
        copy.start()
    for copy in copies:
        copy.wait()


def local(queries, cache_keys, cache_values, new_keys, new_values, lengths, residual, out_weight, norm_gain,
          gate_weight, up_weight, down_weight):
    hbm = pl.BlockSpec(memory_space=pl.ANY)
    vmem = pl.BlockSpec(memory_space=pltpu.VMEM)
    dma = pltpu.SemaphoreType.DMA
    after, layer = pl.pallas_call(
        kernel,
        out_shape=(pltpu.VMEM((KV, COLS), BF16), pltpu.VMEM((4, COLS), BF16)),
        in_specs=[hbm] * 12,
        out_specs=(vmem, vmem),
        scratch_shapes=[
            pltpu.SMEM((SEQS,), jnp.int32),
            pltpu.VMEM((KV, HEADS, HD), BF16),
            pltpu.VMEM((SEQS, CTX, HD), BF16),
            pltpu.VMEM((SEQS, CTX, HD), BF16),
            pltpu.VMEM((SEQS, STEPS, HD), BF16),
            pltpu.VMEM((SEQS, STEPS, HD), BF16),
            pltpu.VMEM((KV, COLS), BF16),
            pltpu.VMEM((HEADS * HD, COLS), BF16),
            pltpu.VMEM((4, 128), BF16),
            pltpu.VMEM((COLS, 2 * FF), BF16),
            pltpu.VMEM((FF, COLS), BF16),
            pltpu.VMEM((KV, HEADS, HD), BF16),
            pltpu.VMEM((SEQS, 1, 128), F32),
            pltpu.VMEM((KV - 1, HEADS, HD), BF16),
            pltpu.VMEM((KV, 1, 128), F32),
            pltpu.VMEM((128, 128), F32),
            pltpu.VMEM((KV, HEADS, HD), BF16),
            pltpu.VMEM((KV * HEADS, HD), F32),
            pltpu.VMEM((TP, KV, COLS), BF16),
            pltpu.VMEM((KV, COLS), F32),
            pltpu.VMEM((KV, 1, 128), F32),
            pltpu.VMEM((Z, Y, 8, 1024), BF16),
            pltpu.VMEM((Z, Y - 1, 8, 1024), BF16),
            pltpu.VMEM((Y, 8, 1024), F32),
            pltpu.VMEM((8, 1024), F32),
            pltpu.VMEM((2, Y, 8, 1024), BF16),
            pltpu.VMEM((Z, 8, 1024), BF16),
            pltpu.VMEM((Z - 3, 8, 1024), BF16),
            pltpu.VMEM((Z, Y, 8, 512), BF16),
            pltpu.VMEM((2414, 1, 128), F32),
            pltpu.VMEM((4, 8, COLS), BF16),
            pltpu.VMEM((TP - 1, 8, COLS), BF16),
            dma((7,)), dma, dma, dma((2,)), dma, dma, dma, dma((len(Y_STAGE),)), dma, dma, dma, dma,
        ],
        compiler_params=pltpu.CompilerParams(
            collective_id=0, has_side_effects=True, vmem_limit_bytes=60 * 1024 * 1024
        ),
    )(
        *(
            pltpu.with_memory_space_constraint(array, pltpu.HBM)
            for array in (
                lengths,
                queries.reshape(KV, HEADS, HD),
                cache_keys.reshape(SEQS, CTX, HD),
                cache_values.reshape(SEQS, CTX, HD),
                new_keys.reshape(SEQS, STEPS, HD),
                new_values.reshape(SEQS, STEPS, HD),
                residual,
                out_weight,
                norm_gain.reshape(4, 128),
                gate_weight,
                up_weight,
                down_weight,
            )
        )
    )
    return pl.pallas_call(
        write_out,
        out_shape=(jax.ShapeDtypeStruct((KV, COLS), BF16), jax.ShapeDtypeStruct((4, COLS), BF16)),
        in_specs=[vmem, vmem],
        out_specs=(hbm, hbm),
        scratch_shapes=[dma((2,))],
        compiler_params=pltpu.CompilerParams(vmem_limit_bytes=1024 * 1024),
    )(after, layer)


def solution(mesh):
    return jax.shard_map(
        local,
        mesh=mesh,
        in_specs=(
            P(None, None, "tp", None),
            P(None, "kv", "tp", None),
            P(None, "kv", "tp", None),
            P(None, None, "tp", None),
            P(None, None, "tp", None),
            P(),
            P(None, "kv"),
            P("tp", "kv"),
            P("kv"),
            P("kv", "tp"),
            P("kv", "tp"),
            P("tp", "kv"),
        ),
        out_specs=(P(None, "kv"), P("tp", "kv")),
        check_vma=False,
    )
```

```python
import math

import jax
import jax.numpy as jnp
from jax import lax
from jax.experimental import pallas as pl
from jax.experimental.pallas import tpu as pltpu
from jax.sharding import PartitionSpec as P

F32, BF16 = jnp.float32, jnp.bfloat16
MESH = pl.DeviceIdType.MESH
Z, Y, TP = 8, 4, 8
KV = Z * Y
SEQS, STEPS, HEADS, HD = 8, 4, 16, 128
CTX = 256
COLS = 512
MODEL = 16384
FF = 3328
WIDTH = (3, 3, 3, 3, 3, 3, 4, 4)
FAR_FIRST = (4, 3, 5, 2, 6, 1, 7, 0)
NEAR = (1, 7)
Y_STAGE = (4, 3, 5, 2, 6, 0)
HOPS = lambda o: min(o[0], Z - o[0]) + min(o[1], Y - o[1])
OTHERS = sorted(((d, e) for d in range(Z) for e in range(Y) if d or e), key=HOPS, reverse=True)


def slot_of(d, e):
    return (Z - d) % Z * Y + (Y - e) % Y - 1


SCALE = 1.0 / math.sqrt(HD)
LOW = -1e30


def drain(ref, sem):
    pltpu.make_async_copy(ref, ref, sem).wait()


def by_width(c, body):
    @pl.when(c < 6)
    def _():
        body(3)

    @pl.when(c >= 6)
    def _():
        body(4)


def kernel(
    lengths_in,
    q_in, k_in, v_in, nk_in, nv_in, res_in, wo_in, gain_in, wg_in, wu_in, wd_in,
    after_out, layer_out,
    lengths, qv, kb, vb, nkb, nvb, resb, wo, gainb, wgu, wd,
    obuf, sbuf, ra, rs, tb, gb, gf, pr, aft,
    sq, yb, yr, own_part, own_sum, nr, zs, zr, hr, sized, fs, fr,
    load_sem, gu_sem, sent, a_recv, b_recv, c_recv, sq_recv, y_recv, n_recv, z_recv, h_recv, f_recv,
):
    kv, tp = lax.axis_index("kv"), lax.axis_index("tp")
    z, y = kv // Y, kv % Y
    x, core = tp // 2, tp % 2

    pairs = (
        (lengths_in, lengths), (q_in, qv), (k_in, kb), (v_in, vb), (nk_in, nkb), (nv_in, nvb), (res_in, resb), (gain_in, gainb),
        (wo_in, wo), (wd_in, wd),
    )
    loads = [pltpu.make_async_copy(a, b, load_sem.at[i]) for i, (a, b) in zip((0, 1, 1, 1, 2, 2, 3, 4, 5, 6), pairs)]

    def send(src, dst, send_sem, recv_sem, to):
        pltpu.make_async_remote_copy(
            src_ref=src, dst_ref=dst, send_sem=send_sem, recv_sem=recv_sem, device_id=to, device_id_type=MESH
        ).start()

    def of_plane(d, e):
        return lax.rem(z + d, Z) * Y + lax.rem(y + e, Y)

    for copy in loads[:4]:
        copy.start()
    barrier = pltpu.get_barrier_semaphore()

    @pl.loop(0, KV - 1)
    def _(i):
        j = i // Y
        d = 4 + j // 2 - j % 2 * (j // 2 * 2 + 1)
        pl.semaphore_signal(barrier, inc=1, device_id=(of_plane(d, (i + 1) % Y), tp), device_id_type=MESH)

    @pl.loop(1, TP)
    def _(i):
        pl.semaphore_signal(barrier, inc=1, device_id=(kv, lax.rem(tp + i, TP)), device_id_type=MESH)

    for copy in loads[4:]:
        copy.start()

    loads[0].wait()
    drain(wgu.at[:, 0:1152], load_sem.at[1])
    position = lax.broadcasted_iota(jnp.int32, (STEPS * HEADS, CTX), 1) + kv * CTX
    lane = lax.broadcasted_iota(jnp.int32, (128, 128), 1)
    stats = jnp.zeros((128, 128), F32)
    for s in range(SEQS):
        rows = qv[s * STEPS : (s + 1) * STEPS].reshape(STEPS * HEADS, HD)
        scores = lax.dot_general(rows, kb[s], (((1,), (1,)), ((), ())), preferred_element_type=F32) * SCALE
        inside = position < lengths[s]
        scores = jnp.where(inside, scores, LOW)
        top = jnp.max(scores, axis=1, keepdims=True)
        weights = jnp.where(inside, jnp.exp(scores - top), 0.0)
        total = jnp.sum(weights, axis=1, keepdims=True)
        sums = jnp.dot(weights.astype(BF16), vb[s], preferred_element_type=F32)
        obuf[s * STEPS : (s + 1) * STEPS] = sums.reshape(STEPS, HEADS, HD).astype(BF16)
        stats = jnp.where(lane == s, jnp.concatenate([top, total], axis=0), stats)
    turned = stats.T
    for s in range(SEQS):
        sbuf[s] = turned[s : s + 1]

    pl.semaphore_wait(barrier, KV - 1 + TP - 1)

    for d, e in OTHERS:
        to = of_plane(d, e)
        send(sbuf.at[to // Y], rs.at[slot_of(d, e)], sent, a_recv.at[0], (to, tp))
        send(obuf.at[to], ra.at[slot_of(d, e)], sent, a_recv.at[1], (to, tp))

    @pl.loop(0, FF // 128)
    def _(j):
        block = pl.ds(pl.multiple_of(j * 128, 128), 128)
        for half, weight in enumerate((wg_in, wu_in)):
            there = pl.ds(pl.multiple_of(j * 256 + half * 128, 128), 128)
            pltpu.make_async_copy(weight.at[:, block], wgu.at[:, there], gu_sem).start()

    drain(qv.at[0:4], load_sem.at[2])
    for copy in loads[6:]:
        copy.wait()
    own_q = qv[kv].astype(F32)
    fresh_k, fresh_v = nkb[z].astype(F32), nvb[z].astype(F32)
    fresh = []
    for u in range(STEPS):
        score = jnp.sum(own_q * fresh_k[u : u + 1], axis=1, keepdims=True) * SCALE
        fresh.append(jnp.where(u <= y, score, LOW))
    rs[KV - 1] = sbuf[z]
    drain(rs.at[0 : KV - 1], a_recv.at[0])
    drain(ra, a_recv.at[1])
    tb[:, 0:KV] = rs[...].reshape(KV, 128).T
    tops = tb[pl.ds(pl.multiple_of(y * HEADS, HEADS), HEADS), 0:KV]
    totals = tb[pl.ds(pl.multiple_of(64 + y * HEADS, HEADS), HEADS), 0:KV]
    row_max = jnp.max(tops, axis=1, keepdims=True)
    for score in fresh:
        row_max = jnp.maximum(row_max, score)
    factor = jnp.exp(tops - row_max)
    denominator = jnp.sum(factor * totals, axis=1, keepdims=True)
    numerator = factor[:, KV - 1 : KV] * obuf[kv].astype(F32)
    for u in range(STEPS):
        weight = jnp.where(u <= y, jnp.exp(fresh[u] - row_max), 0.0)
        denominator += weight
        numerator += weight.astype(BF16).astype(F32) * fresh_v[u : u + 1]
    for j in range(KV - 1):
        numerator += factor[:, j : j + 1] * ra[j].astype(F32)
    gb[kv] = (numerator / denominator).astype(BF16)

    for d, e in OTHERS:
        send(gb.at[kv], gb.at[kv], sent, b_recv, (of_plane(d, e), tp))

    drain(gb.at[0 : KV - 1], b_recv)
    gf[...] = gb[...].astype(F32).reshape(KV * HEADS, HD)
    attended = jnp.concatenate(
        [gf[pl.ds(h, KV, stride=HEADS), :].astype(BF16) for h in range(HEADS)], axis=1
    )
    pr[tp] = jnp.dot(attended, wo[...], preferred_element_type=F32).astype(BF16)
    for i in FAR_FIRST[:-1]:
        send(pr.at[tp], pr.at[tp], sent, c_recv, (kv, lax.rem(tp + i, TP)))

    drain(pr.at[0 : TP - 1], c_recv)
    summed = resb[...].astype(F32)
    for t in range(TP):
        summed += pr[t].astype(F32)
    after = summed.astype(BF16)
    wide = after.astype(F32)
    aft[...] = wide
    after_out[...] = after

    normed = jnp.concatenate(
        [wide[:, j * 128 : (j + 1) * 128] * gainb[j : j + 1].astype(F32) for j in range(COLS // 128)], axis=1
    ).astype(BF16)

    def send_squares():
        squares = jnp.broadcast_to(jnp.sum(wide * wide, axis=1, keepdims=True), (KV, 128)).T
        sq[KV - 1, :, 0:KV] = squares[0:1]
        for d, e in OTHERS:
            send(sq.at[KV - 1], sq.at[slot_of(d, e)], sent, sq_recv, (of_plane(d, e), tp))

    def send_y(d, n):
        for e in (2, 1, 3):
            send(
                yb.at[d, lax.rem(y + e, Y), :, 0 : n * 256],
                yr.at[d, Y - 1 - e, :, 0 : n * 256],
                sent,
                y_recv.at[Y_STAGE.index(d)],
                (of_plane(0, e), tp),
            )

    def add_near(n):
        drain(nr.at[:, :, :, 0 : n * 256], n_recv)
        part = own_part[:, :, 0 : n * 256] + nr[0, :, :, 0 : n * 256].astype(F32) + nr[1, :, :, 0 : n * 256].astype(F32)
        own_part[:, :, 0 : n * 256] = part
        yb[0, :, :, 0 : n * 256] = part.astype(BF16)
        send_y(0, n)

    def multiply(d):
        c = lax.rem(z + d, Z)

        def body(n):
            block = pl.ds(pl.multiple_of(c * 768 + jnp.maximum(c - 6, 0) * 256, 256), n * 256)
            both = jnp.dot(normed, wgu[:, block], preferred_element_type=F32).reshape(Y, 8, n * 256)
            if d == 0:
                own_part[:, :, 0 : n * 256] = both
            else:
                yb[d, :, :, 0 : n * 256] = both.astype(BF16)
            if d in NEAR:
                send(
                    yb.at[d, :, :, 0 : n * 256],
                    nr.at[NEAR.index(d), :, :, 0 : n * 256],
                    sent,
                    n_recv,
                    (of_plane(d, 0), tp),
                )
            elif d:
                send_y(d, n)

        by_width(c, body)

    drain(wgu, gu_sem)
    for d in (4, 3, 5, 1, 7, 2, 6, 0):
        multiply(d)
        if d == 6:
            send_squares()

    def finish_y(d):
        c = lax.rem(z + d, Z)

        def body(n):
            n = n * 256
            drain(yr.at[d, :, :, 0:n], y_recv.at[Y_STAGE.index(d)])
            part = yb[d, y, :, 0:n].astype(F32) if d else own_part[y, :, 0:n]
            for i in range(Y - 1):
                part += yr[d, i, :, 0:n].astype(F32)
            if d == 0:
                own_sum[:, 0:n] = part
            else:
                zs[d, :, 0:n] = part.astype(BF16)
                send(zs.at[d, :, 0:n], zr.at[6 - d, :, 0:n], sent, z_recv, (of_plane(d, 0), tp))

        by_width(c, body)

    for d in (4, 3, 5):
        finish_y(d)
    by_width(z, add_near)
    for d in (2, 6, 0):
        finish_y(d)

    drain(sq.at[0 : KV - 1], sq_recv)
    tb[...] = jnp.broadcast_to(jnp.sum(sq[...].reshape(KV, 128), axis=0, keepdims=True), (128, 128)).T
    inverse = lax.rsqrt(tb[pl.ds(pl.multiple_of(y * 8, 8), 8), :] / MODEL + 1e-05)

    by_width(z, lambda n: drain(zr.at[:, :, 0 : n * 256], z_recv))
    both = own_sum[...]
    for i in range(Z - 3):
        both += zr[i].astype(F32)
    for j in range(4):
        gate = both[:, j * 256 : j * 256 + 128] * inverse
        up = both[:, j * 256 + 128 : j * 256 + 256] * inverse
        hr[z, y, :, j * 128 : (j + 1) * 128] = (gate / (1.0 + jnp.exp(-gate)) * up).astype(BF16)

    def send_hidden(n):
        own = hr.at[z, y, :, 0 : n * 128]
        for d, e in OTHERS:
            send(own, own, sent, h_recv, (of_plane(d, e), tp))

    by_width(z, send_hidden)

    by_width(z, lambda n: drain(sized.at[0 : (Y * sum(WIDTH) - n) * 4], h_recv))
    hidden = jnp.concatenate(
        [hr[c, :, :, 0 : WIDTH[c] * 128].astype(F32).reshape(KV, WIDTH[c] * 128).astype(BF16) for c in range(Z)], axis=1
    )
    down = jnp.dot(hidden, wd[...], preferred_element_type=F32)
    fs[...] = down.reshape(TP, 4, COLS).astype(BF16)

    for i in FAR_FIRST[:-1]:
        to = lax.rem(tp + i, TP)
        send(fs.at[to], fr.at[TP - 1 - i], sent, f_recv, (kv, to))

    wide = aft[pl.ds(pl.multiple_of(x * 8, 8), 8), :]
    rows = jnp.where(core == 0, wide[0:4], wide[4:8]) + fs[tp].astype(F32)
    drain(fr, f_recv)
    for i in range(TP - 1):
        rows += fr[i].astype(F32)
    layer_out[...] = rows.astype(BF16)

    def left(n):
        units = (KV - 1) * (1 + 8 + 8 + 1 + 4 * n) + (TP - 1) * (64 + 8) + (Y * sum(WIDTH) - n) * 8
        drain(sized.at[0:units], sent)

    by_width(z, left)


def write_out(after_in, layer_in, after_out, layer_out, sem):
    copies = [
        pltpu.make_async_copy(after_in, after_out, sem.at[0]),
        pltpu.make_async_copy(layer_in, layer_out, sem.at[1]),
    ]
    for copy in copies:
        copy.start()
    for copy in copies:
        copy.wait()


def local(queries, cache_keys, cache_values, new_keys, new_values, lengths, residual, out_weight, norm_gain,
          gate_weight, up_weight, down_weight):
    hbm = pl.BlockSpec(memory_space=pl.ANY)
    vmem = pl.BlockSpec(memory_space=pltpu.VMEM)
    dma = pltpu.SemaphoreType.DMA
    after, layer = pl.pallas_call(
        kernel,
        out_shape=(pltpu.VMEM((KV, COLS), BF16), pltpu.VMEM((4, COLS), BF16)),
        in_specs=[hbm] * 12,
        out_specs=(vmem, vmem),
        scratch_shapes=[
            pltpu.SMEM((SEQS,), jnp.int32),
            pltpu.VMEM((KV, HEADS, HD), BF16),
            pltpu.VMEM((SEQS, CTX, HD), BF16),
            pltpu.VMEM((SEQS, CTX, HD), BF16),
            pltpu.VMEM((SEQS, STEPS, HD), BF16),
            pltpu.VMEM((SEQS, STEPS, HD), BF16),
            pltpu.VMEM((KV, COLS), BF16),
            pltpu.VMEM((HEADS * HD, COLS), BF16),
            pltpu.VMEM((4, 128), BF16),
            pltpu.VMEM((COLS, 2 * FF), BF16),
            pltpu.VMEM((FF, COLS), BF16),
            pltpu.VMEM((KV, HEADS, HD), BF16),
            pltpu.VMEM((SEQS, 1, 128), F32),
            pltpu.VMEM((KV - 1, HEADS, HD), BF16),
            pltpu.VMEM((KV, 1, 128), F32),
            pltpu.VMEM((128, 128), F32),
            pltpu.VMEM((KV, HEADS, HD), BF16),
            pltpu.VMEM((KV * HEADS, HD), F32),
            pltpu.VMEM((TP, KV, COLS), BF16),
            pltpu.VMEM((KV, COLS), F32),
            pltpu.VMEM((KV, 1, 128), F32),
            pltpu.VMEM((Z, Y, 8, 1024), BF16),
            pltpu.VMEM((Z, Y - 1, 8, 1024), BF16),
            pltpu.VMEM((Y, 8, 1024), F32),
            pltpu.VMEM((8, 1024), F32),
            pltpu.VMEM((2, Y, 8, 1024), BF16),
            pltpu.VMEM((Z, 8, 1024), BF16),
            pltpu.VMEM((Z - 3, 8, 1024), BF16),
            pltpu.VMEM((Z, Y, 8, 512), BF16),
            pltpu.VMEM((2414, 1, 128), F32),
            pltpu.VMEM((TP, 4, COLS), BF16),
            pltpu.VMEM((TP - 1, 4, COLS), BF16),
            dma((7,)), dma, dma, dma((2,)), dma, dma, dma, dma((len(Y_STAGE),)), dma, dma, dma, dma,
        ],
        compiler_params=pltpu.CompilerParams(
            collective_id=0, has_side_effects=True, vmem_limit_bytes=60 * 1024 * 1024
        ),
    )(
        *(
            pltpu.with_memory_space_constraint(array, pltpu.HBM)
            for array in (
                lengths,
                queries.reshape(KV, HEADS, HD),
                cache_keys.reshape(SEQS, CTX, HD),
                cache_values.reshape(SEQS, CTX, HD),
                new_keys.reshape(SEQS, STEPS, HD),
                new_values.reshape(SEQS, STEPS, HD),
                residual,
                out_weight,
                norm_gain.reshape(4, 128),
                gate_weight,
                up_weight,
                down_weight,
            )
        )
    )
    return pl.pallas_call(
        write_out,
        out_shape=(jax.ShapeDtypeStruct((KV, COLS), BF16), jax.ShapeDtypeStruct((4, COLS), BF16)),
        in_specs=[vmem, vmem],
        out_specs=(hbm, hbm),
        scratch_shapes=[dma((2,))],
        compiler_params=pltpu.CompilerParams(vmem_limit_bytes=1024 * 1024),
    )(after, layer)


def solution(mesh):
    return jax.shard_map(
        local,
        mesh=mesh,
        in_specs=(
            P(None, None, "tp", None),
            P(None, "kv", "tp", None),
            P(None, "kv", "tp", None),
            P(None, None, "tp", None),
            P(None, None, "tp", None),
            P(),
            P(None, "kv"),
            P("tp", "kv"),
            P("kv"),
            P("kv", "tp"),
            P("kv", "tp"),
            P("tp", "kv"),
        ),
        out_specs=(P(None, "kv"), P("tp", "kv")),
        check_vma=False,
    )
```
